256 devices in a mesh: hist: 4 (over x), ka: 64 (over z, y, core).
Axes of the slice: x: 4, y: 4, z: 8, core: 2. Of those that a mesh axis runs over, the one named last changes fastest.
Arguments:
- g_row: float32 [2, 16, 128, 1024], P(None, None, None, 'ka'), may hold values from -6 to 6
- w_row: float32 [2, 16, 128, 1024], P(None, None, None, 'ka'), may hold values from -192 to 192
- g_hist: bfloat16 [2, 16, 1024, 128, 128], P(None, None, 'ka', 'hist'), may hold values from -6 to 6
- s_hist: bfloat16 [2, 16, 1024, 128, 128], P(None, None, 'ka', 'hist'), may hold values from -6 to 6
- step_now: int32 [1], replicated, may hold values from 64 to 128
Outputs:
- memory_integral: float32 [2, 16, 1024, 128], P(None, None, 'ka', 'hist')
The draws below stay inside these ranges and needn't reach their ends.
All inputs are finite; a program needn't handle non-finite values.
Results may differ from the reference program's by a relative error of at most 0.0029.
Values may be sent and summed in bfloat16 or wider, within the bound.
A program may use at most 128 MiB of HBM per device.

```python
import jax
import jax.numpy as jnp
from jax import lax

LX = 32
NK = 1024
NORB = 4
PAIRS = 16
TT = 128


def steps_of(own_key, extent, shards, low, top_value):
    loudness = 1.0
    for position, parts in shards:
        draws = jax.random.uniform(jax.random.fold_in(jax.random.fold_in(own_key, 6), position), (parts,), jnp.float32, low / len(shards), top_value / len(shards))
        loudness = loudness * jnp.repeat(jnp.exp(draws), extent[position] // parts).reshape((-1,) + (1,) * (len(extent) - 1 - position))
    return loudness


def scatter_about(own_key, extent, scale, limit, cuts=(), kind=jnp.bfloat16):
    drawn = jax.random.normal(own_key, extent, jnp.float32) * scale
    if len(cuts) > 0:
        drawn = steps_of(own_key, extent, cuts, -0.22, 0.18) * drawn
    return jnp.clip(drawn, min=-limit, max=limit).astype(kind)


def setup_inputs(seed: int = 0) -> dict:
    seeds = jax.random.split(jax.random.key(seed), 6)
    return {
        "g_row": scatter_about(seeds[0], (2, PAIRS, TT, NK), 1.0, 6.0, ((3, 64),), jnp.float32),
        "w_row": scatter_about(seeds[1], (2, PAIRS, TT, NK), LX, 192.0, ((3, 64),), jnp.float32),
        "g_hist": scatter_about(seeds[2], (2, PAIRS, NK, TT, TT), 1.0, 6.0, ((2, 64), (3, 4))),
        "s_hist": scatter_about(seeds[3], (2, PAIRS, NK, TT, TT), 1.0, 6.0, ((2, 64), (3, 4))),
        "step_now": jax.random.randint(seeds[4], (1,), TT // 2, TT + 1).astype(jnp.int32),
    }


def complex_contract(left, right):
    first = left.reshape(2, NORB, NORB, left.shape[2], left.shape[3])
    second = right.reshape(2, NORB, NORB, right.shape[2], right.shape[3], right.shape[4])

    def inner(x, y):
        return jnp.einsum('absk,bcksu->acku', x, y)

    real = inner(first[0], second[0]) - inner(first[1], second[1])
    imag = inner(first[0], second[1]) + inner(first[1], second[0])
    return jnp.stack([real, imag]).reshape(2, NORB * NORB, right.shape[2], right.shape[4])


def reference(g_row, w_row, g_hist, s_hist, step_now):
    green = (g_row[0] + 1j * g_row[1]).reshape(PAIRS, TT, LX, LX)
    screen = (w_row[0] + 1j * w_row[1]).reshape(PAIRS, TT, LX, LX)
    conv = jnp.fft.fft2(jnp.fft.ifft2(green, axes=(2, 3)) * jnp.fft.ifft2(screen, axes=(2, 3)), axes=(2, 3))
    conv = conv.reshape(PAIRS, TT, NK)
    sigma_row = jnp.stack([-conv.imag, conv.real]).astype(jnp.bfloat16)
    g_half = g_row.astype(jnp.bfloat16)
    times = jnp.arange(TT, dtype=jnp.int32)
    live = (times < step_now[0]).astype(jnp.float32)[None, None, :, None]
    live_sigma = sigma_row.astype(jnp.float32) * live
    live_g = g_half.astype(jnp.float32) * live
    lower = times[:, None] >= times[None, :]

    def block(index):
        begin = (index * LX).astype(jnp.int32)
        hist_g = lax.dynamic_slice_in_dim(g_hist, begin, LX, 2).astype(jnp.float32)
        hist_s = lax.dynamic_slice_in_dim(s_hist, begin, LX, 2).astype(jnp.float32)
        hist_g = jnp.where(lower, hist_g, jnp.float32(0.0))
        hist_s = jnp.where(lower, hist_s, jnp.float32(0.0))
        left_sigma = lax.dynamic_slice_in_dim(live_sigma, begin, LX, 3)
        left_green = lax.dynamic_slice_in_dim(live_g, begin, LX, 3)
        return complex_contract(left_sigma, hist_g) + complex_contract(left_green, hist_s)

    pieces = lax.map(block, jnp.arange(LX, dtype=jnp.int32))
    memory = jnp.transpose(pieces, (1, 2, 0, 3, 4)).reshape(2, PAIRS, NK, TT)
    return memory * (2.0 / TT)
```

```python
import functools
import math

import jax
import jax.numpy as jnp
import ml_dtypes
import numpy as np
from jax import lax
from jax.experimental import pallas as pl
from jax.experimental.pallas import tpu as pltpu
from jax.sharding import PartitionSpec as P

LX = 32
NORB = 4
PAIRS = 16
MESH = pl.DeviceIdType.MESH
F32 = jnp.float32
BF16 = jnp.bfloat16


def split_table(table):
    high = table.astype(ml_dtypes.bfloat16)
    low = (table - high.astype(np.float64)).astype(ml_dtypes.bfloat16)
    return high, low


def tables():
    step = np.arange(LX)
    theta = 2.0 * math.pi * (step[:, None] * step[None, :] % LX) / LX
    cosine, sine = np.cos(theta), np.sin(theta)
    first = np.block([[cosine, sine], [-sine, cosine]])
    high, low = split_table(first)
    first = np.concatenate([high, low, high], axis=1)
    last = np.stack(
        [np.concatenate([-sine, -cosine], 1), np.concatenate([cosine, -sine], 1)],
        axis=1,
    ).reshape(2 * LX, 2 * LX) / float(LX**4)
    high, low = split_table(last)
    last = np.concatenate([high, low, high], axis=1)
    eye = np.eye(8)

    def along(table):
        cut = table.reshape(2, 16, LX)
        return np.einsum("hky,pq->hpkqy", cut, eye).reshape(256, 256)

    forth = np.concatenate([along(cosine), along(sine)], axis=1)
    back = np.concatenate([along(cosine).T, along(sine).T], axis=1)
    return (first, last) + split_table(forth) + split_table(back)


def cut(value):
    high = value.astype(BF16)
    low = (value - high.astype(F32)).astype(BF16)
    return high, low


def dot(left, right):
    return jnp.dot(left, right, preferred_element_type=F32)


def fine_dot(left, right_high, right_low):
    rows = left.shape[0]
    high, low = cut(left)
    both = dot(jnp.concatenate([high, low], axis=0), right_high)
    return both[:rows] + both[rows:] + dot(high, right_low)


def four(i):
    return pl.ds(pl.multiple_of(4 * i, 4), 4)


def convolve(block, first, last, forth, back):
    data = jnp.concatenate(
        [
            jnp.concatenate([block(a, 0, half), block(a, 1, half)], axis=0)
            for a in range(2)
            for half in range(2)
        ],
        axis=1,
    )
    high, low = cut(data)
    stage = dot(first, jnp.concatenate([high, high, low], axis=0))
    stage = jnp.concatenate([stage[:, :256], stage[:, 256:]], axis=0)
    stage = fine_dot(stage, *forth)
    parts = []
    for a in range(2):
        re, im = stage[64 * a : 64 * a + 32], stage[64 * a + 32 : 64 * a + 64]
        parts.append((re[:, :256] + im[:, 256:], im[:, :256] - re[:, 256:]))
    (g_re, g_im), (w_re, w_im) = parts
    prod = jnp.concatenate([g_re * w_re - g_im * w_im, g_re * w_im + g_im * w_re], axis=0)
    stage = fine_dot(prod, *back)
    re, im = stage[:32], stage[32:]
    stage = jnp.concatenate([re[:, :256] - im[:, 256:], im[:, :256] + re[:, 256:]], axis=0)
    high, low = cut(stage)
    return dot(last, jnp.concatenate([high, high, low], axis=0))


def kernel(
    n_ka, n_hist,
    step_ref, g_hbm, w_hbm, gh_hbm, sh_hbm, first_hbm, last_hbm, fh_hbm, fl_hbm, bh_hbm, bl_hbm,
    out_ref,
    rows_v, gh_v, sh_v, first_v, last_v, fh_v, fl_v, bh_v, bl_v,
    turned, send_rows, recv_rows, send_sig, recv_sig, wide_sig, left_g, left_s, partial, rs_send, rs_recv, summed,
    row_sem, table_sem, sh_sem, gh_sem, self_sem, send_sem, recv_sem,
):
    hist = lax.axis_index("hist")
    me = lax.axis_index("ka")
    slab = LX

    row_copies = [
        pltpu.make_async_copy(g_hbm, rows_v.at[0], row_sem.at[0]),
        pltpu.make_async_copy(w_hbm, rows_v.at[1], row_sem.at[1]),
    ]
    for copy in row_copies:
        copy.start()

    barrier = pltpu.get_barrier_semaphore()

    def greet(i, carry):
        pl.semaphore_signal(barrier, inc=1, device_id={"ka": lax.rem(me + i, n_ka)}, device_id_type=MESH)
        return carry

    lax.fori_loop(1, n_ka, greet, 0)
    for d in range(1, n_hist):
        pl.semaphore_signal(barrier, inc=1, device_id={"hist": lax.rem(hist + d, n_hist)}, device_id_type=MESH)

    table_copies = [
        pltpu.make_async_copy(src, dst, table_sem.at[i])
        for i, (src, dst) in enumerate(
            [(first_hbm, first_v), (last_hbm, last_v), (fh_hbm, fh_v), (fl_hbm, fl_v), (bh_hbm, bh_v), (bl_hbm, bl_v)]
        )
    ]
    chunks = 4
    width = 16 // chunks
    sh_copies = [
        pltpu.make_async_copy(
            sh_hbm.at[:, :, pl.ds(q * width, width)], sh_v.at[:, :, pl.ds(q * width, width)], sh_sem.at[q]
        )
        for q in range(chunks)
    ]
    gh_copies = [
        pltpu.make_async_copy(
            gh_hbm.at[:, :, pl.ds(q * width, width)], gh_v.at[:, :, pl.ds(q * width, width)], gh_sem.at[q]
        )
        for q in range(chunks)
    ]
    for copy in table_copies + sh_copies + gh_copies:
        copy.start()

    for copy in row_copies:
        copy.wait()
    for a in range(2):
        for part in range(2):
            r = 2 * a + part
            for ph in range(2):
                turned[2 * r + ph] = rows_v[a, part, pl.ds(128 * ph, 128), :].T
    for r in range(4):
        for ph in range(2):
            send_rows[pl.ds(4 * ph + r, 32, stride=8), :] = turned[2 * r + ph, pl.ds(slab * hist, slab), :]

    pl.semaphore_wait(barrier, n_ka - 1 + n_hist - 1)

    def send_row(i, carry):
        to = lax.rem(me + i, n_ka)
        pltpu.make_async_remote_copy(
            src_ref=send_rows.at[four(to)], dst_ref=recv_rows.at[four(me)], send_sem=send_sem.at[0], recv_sem=recv_sem.at[0],
            device_id={"ka": to}, device_id_type=MESH,
        ).start()
        return carry

    lax.fori_loop(1, n_ka, send_row, 0)
    own_row = pltpu.make_async_copy(send_rows.at[four(me)], recv_rows.at[four(me)], self_sem.at[0])
    own_row.start()

    lane = lax.broadcasted_iota(jnp.int32, (1, 128), 1)
    place = lane // 32
    alive = (hist * slab + lane % 32) < step_ref[0]

    def spread(left, pieces):
        for part in range(2):
            for a in range(NORB):
                row = pieces(part, a, 0)
                for b in range(1, NORB):
                    row = jnp.where(place == b, pieces(part, a, b), row)
                row = jnp.where(alive, row, 0.0)
                if part == 0:
                    left[0, pl.ds(a, 16, stride=8), :] = row
                    left[1, pl.ds(4 + a, 16, stride=8), :] = row
                else:
                    left[1, pl.ds(a, 16, stride=8), :] = -row
                    left[0, pl.ds(4 + a, 16, stride=8), :] = row

    def green_piece(part, a, b):
        block = rows_v[0, part, pl.ds((4 * a + b) * 16, 16), :]
        return pltpu.roll(block, lax.rem(32 * b + 128 - 32 * hist, 128), 1)

    spread(left_g, green_piece)

    def left_of(left, k):
        at = pl.ds(8 * k, 8)
        return jnp.concatenate([left[0, at, :], left[1, at, :]], axis=1).astype(BF16)

    s_at = lax.broadcasted_iota(jnp.int32, (slab, 128), 0) + hist * slab
    t_at = lax.broadcasted_iota(jnp.int32, (slab, 128), 1)
    lower = jnp.where(s_at >= t_at, 1.0, 0.0).astype(BF16)

    def history(ref, k):
        return jnp.concatenate(
            [
                jnp.concatenate(
                    [ref[part, 4 * b + c, k] * lower for part in range(2) for b in range(NORB)], axis=0
                )
                for c in range(NORB)
            ],
            axis=1,
        )

    for q in range(chunks):
        sh_copies[q].wait()
        for kk in range(width):
            k = q * width + kk
            partial[k] = dot(left_of(left_g, k), history(sh_v, k))

    for copy in table_copies:
        copy.wait()
    own_row.wait()
    rest = recv_rows.at[pl.ds(0, 4 * (n_ka - 1))]
    pltpu.make_async_copy(rest, rest, recv_sem.at[0]).wait()

    def block(a, part, half):
        return recv_rows[pl.ds(4 * half + 2 * a + part, 32, stride=8), :]

    sigma = convolve(block, first_v[...], last_v[...], (fh_v[...], fl_v[...]), (bh_v[...], bl_v[...])).astype(BF16)
    for half in range(2):
        send_sig[half] = sigma[:, 128 * half : 128 * half + 128].reshape(LX, 2, 128)

    time, group = me // 2, lax.rem(me, 2)
    landing = group * LX + time

    def send_sigma(i, carry):
        to = lax.rem(me + i, n_ka)
        pltpu.make_async_remote_copy(
            src_ref=send_sig.at[lax.rem(to, 2), to // 2], dst_ref=recv_sig.at[landing],
            send_sem=send_sem.at[1], recv_sem=recv_sem.at[1], device_id={"ka": to}, device_id_type=MESH,
        ).start()
        return carry

    lax.fori_loop(1, n_ka, send_sigma, 0)
    own_sig = pltpu.make_async_copy(send_sig.at[group, time], recv_sig.at[landing], self_sem.at[1])
    own_sig.start()
    own_sig.wait()
    most = recv_sig.at[pl.ds(0, n_ka - 1)]
    pltpu.make_async_copy(most, most, recv_sem.at[1]).wait()

    wide_sig[...] = recv_sig[...].reshape(2, 2 * LX, 128).astype(F32)
    stacked = jnp.concatenate(
        [wide_sig[ph, pl.ds(part, 32, stride=2), :] for part in range(2) for ph in range(2)], axis=0
    ).T

    def sigma_piece(part, a, b):
        ph = a // 2
        at = ((a % 2) * 4 + b) * 16
        shift = (32 * (b - 2 * part - ph)) % 128
        rows = stacked[at : at + 16]
        return pltpu.roll(rows, shift, 1) if shift else rows

    spread(left_s, sigma_piece)

    for q in range(chunks):
        gh_copies[q].wait()
        for kk in range(width):
            k = q * width + kk
            total = partial[k] + dot(left_of(left_s, k), history(gh_v, k))
            columns = [total[:, 128 * c : 128 * c + 128] for c in range(NORB)]
            for to in range(NORB):
                row = None
                for c in range(NORB):
                    shift = (32 * (c - to)) % 128
                    moved = pltpu.roll(columns[c], shift, 1) if shift else columns[c]
                    row = moved if row is None else jnp.where(place == c, moved, row)
                rs_send[to, k] = row
        for d in range(1, n_hist):
            to = lax.rem(hist + d, n_hist)
            pltpu.make_async_remote_copy(
                src_ref=rs_send.at[to, pl.ds(q * width, width)],
                dst_ref=rs_recv.at[n_hist - 1 - d, pl.ds(q * width, width)],
                send_sem=send_sem.at[2], recv_sem=recv_sem.at[2], device_id={"hist": to}, device_id_type=MESH,
            ).start()

    pltpu.make_async_copy(rs_recv, rs_recv, recv_sem.at[2]).wait()
    scale = 2.0 / (n_hist * slab)
    summed[...] = ((rs_recv[0] + rs_recv[1]) + (rs_recv[2] + rs_send[hist])).reshape(128, 128) * scale
    for m in range(8):
        rows = summed[pl.ds(m, 16, stride=8), :]
        for c in range(NORB):
            moved = pltpu.roll(rows, 128 - 32 * c, 1) if c else rows
            out_ref[m // 4, (m % 4) * 4 + c] = moved[:, :slab]

    pltpu.make_async_copy(rest, rest, send_sem.at[0]).wait()
    pltpu.make_async_copy(most, most, send_sem.at[1]).wait()
    pltpu.make_async_copy(rs_recv, rs_recv, send_sem.at[2]).wait()


def per_device(n_ka, n_hist, g_row, w_row, g_hist, s_hist, step_now):
    rows = [jnp.transpose(x, (0, 1, 3, 2)).reshape(2, PAIRS * 16, 128) for x in (g_row, w_row)]
    first, last, fh, fl, bh, bl = (jnp.asarray(t) for t in tables())
    anywhere = pl.BlockSpec(memory_space=pltpu.HBM)
    return pl.pallas_call(
        functools.partial(kernel, n_ka, n_hist),
        out_shape=jax.ShapeDtypeStruct((2, PAIRS, 16, 32), F32),
        in_specs=[pl.BlockSpec(memory_space=pltpu.SMEM)] + [anywhere] * 10,
        out_specs=pl.BlockSpec(memory_space=pltpu.VMEM),
        scratch_shapes=[
            pltpu.VMEM((2, 2, 256, 128), F32),
            pltpu.VMEM((2, 16, 16, 32, 128), BF16),
            pltpu.VMEM((2, 16, 16, 32, 128), BF16),
            pltpu.VMEM((64, 192), BF16),
            pltpu.VMEM((64, 192), BF16),
            pltpu.VMEM((256, 512), BF16),
            pltpu.VMEM((256, 512), BF16),
            pltpu.VMEM((256, 512), BF16),
            pltpu.VMEM((256, 512), BF16),
            pltpu.VMEM((8, 128, 128), F32),
            pltpu.VMEM((256, 128), F32),
            pltpu.VMEM((256, 128), F32),
            pltpu.VMEM((2, 32, 2, 128), BF16),
            pltpu.VMEM((64, 2, 128), BF16),
            pltpu.VMEM((2, 64, 128), F32),
            pltpu.VMEM((2, 128, 128), F32),
            pltpu.VMEM((2, 128, 128), F32),
            pltpu.VMEM((16, 8, 512), F32),
            pltpu.VMEM((4, 16, 8, 128), F32),
            pltpu.VMEM((3, 16, 8, 128), F32),
            pltpu.VMEM((128, 128), F32),
            pltpu.SemaphoreType.DMA((2,)),
            pltpu.SemaphoreType.DMA((6,)),
            pltpu.SemaphoreType.DMA((4,)),
            pltpu.SemaphoreType.DMA((4,)),
            pltpu.SemaphoreType.DMA((2,)),
            pltpu.SemaphoreType.DMA((3,)),
            pltpu.SemaphoreType.DMA((3,)),
        ],
        compiler_params=pltpu.CompilerParams(
            collective_id=0, has_side_effects=True, vmem_limit_bytes=60 * 1024 * 1024
        ),
    )(step_now, *rows, g_hist, s_hist, first, last, fh, fl, bh, bl)


def solution(mesh):
    placed = (
        P(None, None, None, "ka"),
        P(None, None, None, "ka"),
        P(None, None, "ka", "hist", None),
        P(None, None, "ka", "hist", None),
        P(),
    )
    return jax.shard_map(
        functools.partial(per_device, mesh.shape["ka"], mesh.shape["hist"]),
        mesh=mesh,
        in_specs=placed,
        out_specs=P(None, None, "ka", "hist"),
        check_vma=False,
    )
```

```python
import functools
import math

import jax
import jax.numpy as jnp
import ml_dtypes
import numpy as np
from jax import lax
from jax.experimental import pallas as pl
from jax.experimental.pallas import tpu as pltpu
from jax.sharding import PartitionSpec as P

LX = 32
NORB = 4
LIMIT = 54800
PAIRS = 16
MESH = pl.DeviceIdType.MESH
F32 = jnp.float32
BF16 = jnp.bfloat16


def split_table(table):
    high = table.astype(ml_dtypes.bfloat16)
    low = (table - high.astype(np.float64)).astype(ml_dtypes.bfloat16)
    return high, low


def tables():
    step = np.arange(LX)
    theta = 2.0 * math.pi * (step[:, None] * step[None, :] % LX) / LX
    cosine, sine = np.cos(theta), np.sin(theta)
    first = np.block([[cosine, sine], [-sine, cosine]])
    high, low = split_table(first)
    first = np.concatenate([high, low, high], axis=1)
    last = np.stack(
        [np.concatenate([-sine, -cosine], 1), np.concatenate([cosine, -sine], 1)],
        axis=1,
    ).reshape(2 * LX, 2 * LX) / float(LX**4)
    high, low = split_table(last)
    last = np.concatenate([high, low, high], axis=1)
    eye = np.eye(8)

    def along(table):
        cut = table.reshape(2, 16, LX)
        return np.einsum("hky,pq->hpkqy", cut, eye).reshape(256, 256)

    forth = np.concatenate([along(cosine), along(sine)], axis=1)
    back = np.concatenate([along(cosine).T, along(sine).T], axis=1)
    ends = np.zeros((128, 512), ml_dtypes.bfloat16)
    ends[:64, :192], ends[64:, :192] = first, last
    return np.concatenate(split_table(forth) + split_table(back) + (ends,), axis=0)


def cut(value):
    high = value.astype(BF16)
    low = (value - high.astype(F32)).astype(BF16)
    return high, low


def dot(left, right):
    return jnp.dot(left, right, preferred_element_type=F32)


def fine_dot(left, right_high, right_low):
    rows = left.shape[0]
    high, low = cut(left)
    both = dot(jnp.concatenate([high, low], axis=0), right_high)
    return both[:rows] + both[rows:] + dot(high, right_low)


def convolve(block, table):
    first, last = table[1024:1088, :192], table[1088:1152, :192]
    forth = table[0:256, :], table[256:512, :]
    back = table[512:768, :], table[768:1024, :]
    data = jnp.concatenate(
        [
            jnp.concatenate([block(ph, a, 0, half), block(ph, a, 1, half)], axis=0)
            for ph in range(2)
            for a in range(2)
            for half in range(2)
        ],
        axis=1,
    )
    high, low = cut(data)
    stage = dot(first, jnp.concatenate([high, high, low], axis=0))
    stage = jnp.concatenate([stage[:, 256 * i : 256 * i + 256] for i in range(4)], axis=0)
    stage = fine_dot(stage, *forth)
    prods = []
    for ph in range(2):
        parts = []
        for i in (2 * ph, 2 * ph + 1):
            re, im = stage[64 * i : 64 * i + 32], stage[64 * i + 32 : 64 * i + 64]
            parts.append((re[:, :256] + im[:, 256:], im[:, :256] - re[:, 256:]))
        (g_re, g_im), (w_re, w_im) = parts
        prods += [g_re * w_re - g_im * w_im, g_re * w_im + g_im * w_re]
    stage = fine_dot(jnp.concatenate(prods, axis=0), *back)
    wide = []
    for ph in range(2):
        re, im = stage[64 * ph : 64 * ph + 32], stage[64 * ph + 32 : 64 * ph + 64]
        wide.append(jnp.concatenate([re[:, :256] - im[:, 256:], im[:, :256] + re[:, 256:]], axis=0))
    high, low = cut(jnp.concatenate(wide, axis=1))
    return dot(last, jnp.concatenate([high, high, low], axis=0))


def kernel(
    n_ka, n_hist,
    step_hbm, g_hbm, w_hbm, gh_hbm, sh_hbm, table_hbm,
    out_ref,
    step_ref, rows_v, gh_v, sh_v, table_v,
    turned, send_rows, recv_rows, send_sig, recv_sig, wide_sig, left_g, left_s, partial, rs_full, rs_send, rs_recv, summed,
    row_sem, table_sem, sh_sem, gh_sem, self_sem, send_sem, recv_sem,
):
    hist = lax.axis_index("hist")
    me = lax.axis_index("ka")
    slab = LX
    n_conv = slab
    convolver = me < n_conv
    barrier = pltpu.get_barrier_semaphore()

    row_copies = [
        pltpu.make_async_copy(src.at[part], rows_v.at[a, part], row_sem.at[a, part])
        for a, src in enumerate((g_hbm, w_hbm))
        for part in range(2)
    ]
    for copy in row_copies:
        copy.start()

    @pl.when(convolver)
    def _():
        def greet(i, carry):
            pl.semaphore_signal(barrier, inc=1, device_id={"ka": lax.rem(me + i, n_ka)}, device_id_type=MESH)
            return carry

        lax.fori_loop(1, n_ka, greet, 0)

    for d in range(1, n_hist):
        pl.semaphore_signal(barrier, inc=1, device_id={"hist": lax.rem(hist + d, n_hist)}, device_id_type=MESH)

    step_copy = pltpu.make_async_copy(step_hbm, step_ref, table_sem.at[0])
    table_copy = pltpu.make_async_copy(table_hbm, table_v, table_sem.at[1])
    chunks = 4
    width = 16 // chunks
    sh_copies = [
        pltpu.make_async_copy(
            sh_hbm.at[:, :, pl.ds(q * width, width)], sh_v.at[:, :, pl.ds(q * width, width)], sh_sem.at[q]
        )
        for q in range(chunks)
    ]
    gh_copies = [
        pltpu.make_async_copy(
            gh_hbm.at[:, :, pl.ds(q * width, width)], gh_v.at[:, :, pl.ds(q * width, width)], gh_sem.at[q]
        )
        for q in range(chunks)
    ]
    for copy in [step_copy] + sh_copies + [table_copy] + gh_copies:
        copy.start()

    for a in range(2):
        for part in range(2):
            r = 2 * a + part
            row_copies[r].wait()
            for ph in range(2):
                turned[2 * r + ph] = rows_v[a, part, pl.ds(128 * ph, 128), :].T
    for r in range(4):
        for ph in range(2):
            send_rows[pl.ds(4 * ph + r, slab, stride=8), :] = turned[2 * r + ph, pl.ds(slab * hist, slab), :]

    def tile(i):
        return pl.ds(pl.multiple_of(8 * i, 8), 8)

    def send_row(to):
        pltpu.make_async_remote_copy(
            src_ref=send_rows.at[tile(to)], dst_ref=recv_rows.at[tile(me)], send_sem=send_sem.at[0],
            recv_sem=recv_sem.at[0], device_id={"ka": to}, device_id_type=MESH,
        ).start()

    some_rows = recv_rows.at[pl.ds(0, 8 * (n_conv - 1))]
    all_rows = recv_rows.at[pl.ds(0, 8 * n_conv)]
    other_rows = recv_rows.at[pl.ds(0, 8 * (n_ka - 1))]
    some_sig = recv_sig.at[:, pl.ds(0, n_conv - 1)]

    @pl.when(convolver)
    def _():
        own = pltpu.make_async_copy(send_rows.at[tile(me)], recv_rows.at[tile(me)], self_sem.at[0])
        own.start()
        pl.semaphore_wait(barrier, n_conv - 1 + n_hist - 1)

        def go(i, carry):
            send_row(lax.rem(me + i, n_conv))
            return carry

        lax.fori_loop(1, n_conv, go, 0)
        own.wait()

    @pl.when(jnp.logical_not(convolver))
    def _():
        pl.semaphore_wait(barrier, n_conv + n_hist - 1)

        def go(i, carry):
            send_row(lax.rem(me + i, n_conv))
            return carry

        lax.fori_loop(0, n_conv, go, 0)

    step_copy.wait()
    lane = lax.broadcasted_iota(jnp.int32, (1, 128), 1)
    place = lane // 32
    alive = (hist * slab + lane % 32) < step_ref[0]

    def spread(left, pieces):
        for part in range(2):
            for a in range(NORB):
                row = pieces(part, a, 0)
                for b in range(1, NORB):
                    row = jnp.where(place == b, pieces(part, a, b), row)
                row = jnp.where(alive, row, 0.0)
                left[part, pl.ds(a, 16, stride=8), :] = -row if part else row
                left[1 - part, pl.ds(4 + a, 16, stride=8), :] = row

    def green_piece(part, a, b):
        block = rows_v[0, part, pl.ds((4 * a + b) * 16, 16), :]
        return pltpu.roll(block, lax.rem(32 * b + 128 - 32 * hist, 128), 1)

    def left_of(left, k):
        at = pl.ds(8 * k, 8)
        return jnp.concatenate([left[0, at, :], left[1, at, :]], axis=1).astype(BF16)

    spread(left_g, green_piece)

    s_at = lax.broadcasted_iota(jnp.int32, (slab, 128), 0) + hist * slab
    t_at = lax.broadcasted_iota(jnp.int32, (slab, 128), 1)
    lower = jnp.where(s_at >= t_at, 1.0, 0.0).astype(BF16)

    def history(ref, k):
        return jnp.concatenate(
            [
                jnp.concatenate(
                    [ref[part, 4 * b + c, k] * lower for part in range(2) for b in range(NORB)], axis=0
                )
                for c in range(NORB)
            ],
            axis=1,
        )

    for q in range(chunks):
        sh_copies[q].wait()
        for kk in range(width):
            k = q * width + kk
            partial[k] = dot(left_of(left_g, k), history(sh_v, k))

    table_copy.wait()

    @pl.when(convolver)
    def _():
        pltpu.make_async_copy(other_rows, other_rows, recv_sem.at[0]).wait()

        def block(ph, a, part, half):
            return recv_rows[pl.ds(8 * half + 4 * ph + 2 * a + part, 32, stride=16), :]

        sigma = convolve(block, table_v).astype(BF16)
        for ph in range(2):
            for half in range(2):
                at = 128 * (2 * ph + half)
                send_sig[half, ph] = sigma[:, at : at + 128].reshape(LX, 2, 128)

        def send_sigma(i, carry):
            to = 8 * (i // 8) + lax.rem(me + i, 8)

            @pl.when(to != me)
            def _():
                pltpu.make_async_remote_copy(
                    src_ref=send_sig.at[lax.rem(to, 2), :, to // 2], dst_ref=recv_sig.at[:, me],
                    send_sem=send_sem.at[1], recv_sem=recv_sem.at[1], device_id={"ka": to}, device_id_type=MESH,
                ).start()

            return carry

        lax.fori_loop(0, n_ka, send_sigma, 0)
        own = pltpu.make_async_copy(send_sig.at[lax.rem(me, 2), :, me // 2], recv_sig.at[:, me], self_sem.at[1])
        own.start()
        own.wait()
        pltpu.make_async_copy(some_sig, some_sig, recv_sem.at[1]).wait()

    @pl.when(jnp.logical_not(convolver))
    def _():
        pltpu.make_async_copy(recv_sig, recv_sig, recv_sem.at[1]).wait()

    wide_sig[...] = recv_sig[...].reshape(2, 2 * LX, 128).astype(F32)
    stacked = jnp.concatenate(
        [wide_sig[ph, pl.ds(part, 32, stride=2), :] for part in range(2) for ph in range(2)], axis=0
    ).T

    def sigma_piece(part, a, b):
        ph = a // 2
        at = ((a % 2) * 4 + b) * 16
        shift = (32 * (b - 2 * part - ph)) % 128
        rows = stacked[at : at + 16]
        return pltpu.roll(rows, shift, 1) if shift else rows

    spread(left_s, sigma_piece)

    for q in range(chunks):
        gh_copies[q].wait()
        rows = [[] for _ in range(NORB)]
        for kk in range(width):
            k = q * width + kk
            total = partial[k] + dot(left_of(left_s, k), history(gh_v, k))
            columns = [total[:, 128 * c : 128 * c + 128] for c in range(NORB)]
            for to in range(NORB):
                row = None
                for c in range(NORB):
                    shift = (32 * (c - to)) % 128
                    moved = pltpu.roll(columns[c], shift, 1) if shift else columns[c]
                    row = moved if row is None else jnp.where(place == c, moved, row)
                rows[to].append(row)
        for to in range(NORB):
            full = jnp.concatenate(rows[to], axis=0)
            rs_full[to, q] = full
            rs_send[to, q] = full.astype(BF16)
        for d in (2, 1, 3):
            to = lax.rem(hist + d, n_hist)
            pltpu.make_async_remote_copy(
                src_ref=rs_send.at[to, q], dst_ref=rs_recv.at[n_hist - 1 - d, q],
                send_sem=send_sem.at[2], recv_sem=recv_sem.at[2], device_id={"hist": to}, device_id_type=MESH,
            ).start()

    pltpu.make_async_copy(rs_recv, rs_recv, recv_sem.at[2]).wait()
    scale = 2.0 / (n_hist * slab)
    got = [rs_recv[i].reshape(128, 128).astype(F32) for i in range(3)]
    summed[...] = ((got[0] + got[1]) + (got[2] + rs_full[hist].reshape(128, 128))) * scale
    for m in range(8):
        rows = summed[pl.ds(m, 16, stride=8), :]
        for c in range(NORB):
            moved = pltpu.roll(rows, 128 - 32 * c, 1) if c else rows
            out_ref[m // 4, (m % 4) * 4 + c] = moved[:, :slab]

    pltpu.make_async_copy(rs_recv, rs_recv, send_sem.at[2]).wait()

    @pl.when(convolver)
    def _():
        pltpu.make_async_copy(some_rows, some_rows, send_sem.at[0]).wait()
        pltpu.make_async_copy(recv_sig, recv_sig, send_sem.at[1]).wait()
        pltpu.make_async_copy(some_sig, some_sig, send_sem.at[1]).wait()

    @pl.when(jnp.logical_not(convolver))
    def _():
        pltpu.make_async_copy(all_rows, all_rows, send_sem.at[0]).wait()


def per_device(n_ka, n_hist, g_row, w_row, g_hist, s_hist, step_now):
    rows = [jnp.transpose(x, (0, 1, 3, 2)).reshape(2, PAIRS * 16, 128) for x in (g_row, w_row)]
    table = jnp.asarray(tables())
    return pl.pallas_call(
        functools.partial(kernel, n_ka, n_hist),
        out_shape=jax.ShapeDtypeStruct((2, PAIRS, 16, 32), F32),
        in_specs=[pl.BlockSpec(memory_space=pl.ANY)] * 6,
        out_specs=pl.BlockSpec(memory_space=pltpu.VMEM),
        scratch_shapes=[
            pltpu.SMEM((1,), jnp.int32),
            pltpu.VMEM((2, 2, 256, 128), F32),
            pltpu.VMEM((2, 16, 16, 32, 128), BF16),
            pltpu.VMEM((2, 16, 16, 32, 128), BF16),
            pltpu.VMEM(table.shape, BF16),
            pltpu.VMEM((8, 128, 128), F32),
            pltpu.VMEM((256, 128), F32),
            pltpu.VMEM((512, 128), F32),
            pltpu.VMEM((2, 2, 32, 2, 128), BF16),
            pltpu.VMEM((2, 32, 2, 128), BF16),
            pltpu.VMEM((2, 64, 128), F32),
            pltpu.VMEM((2, 128, 128), F32),
            pltpu.VMEM((2, 128, 128), F32),
            pltpu.VMEM((16, 8, 512), F32),
            pltpu.VMEM((4, 4, 32, 128), F32),
            pltpu.VMEM((4, 4, 32, 128), BF16),
            pltpu.VMEM((3, 4, 32, 128), BF16),
            pltpu.VMEM((128, 128), F32),
            pltpu.SemaphoreType.DMA((2, 2)),
            pltpu.SemaphoreType.DMA((2,)),
            pltpu.SemaphoreType.DMA((4,)),
            pltpu.SemaphoreType.DMA((4,)),
            pltpu.SemaphoreType.DMA((2,)),
            pltpu.SemaphoreType.DMA((3,)),
            pltpu.SemaphoreType.DMA((3,)),
        ],
        compiler_params=pltpu.CompilerParams(
            collective_id=0, has_side_effects=True, vmem_limit_bytes=LIMIT * 1024
        ),
    )(step_now, *rows, g_hist, s_hist, table)


def solution(mesh):
    placed = (
        P(None, None, None, "ka"),
        P(None, None, None, "ka"),
        P(None, None, "ka", "hist", None),
        P(None, None, "ka", "hist", None),
        P(),
    )
    return jax.shard_map(
        functools.partial(per_device, mesh.shape["ka"], mesh.shape["hist"]),
        mesh=mesh,
        in_specs=placed,
        out_specs=P(None, None, "ka", "hist"),
        check_vma=False,
    )
```

```python
import functools
import math

import jax
import jax.numpy as jnp
import ml_dtypes
import numpy as np
from jax import lax
from jax.experimental import pallas as pl
from jax.experimental.pallas import tpu as pltpu
from jax.sharding import PartitionSpec as P

LX = 32
NORB = 4
LIMIT = 54800
PAIRS = 16
MESH = pl.DeviceIdType.MESH
F32 = jnp.float32
BF16 = jnp.bfloat16


def split_table(table):
    high = table.astype(ml_dtypes.bfloat16)
    low = (table - high.astype(np.float64)).astype(ml_dtypes.bfloat16)
    return high, low


def tables():
    step = np.arange(LX)
    theta = 2.0 * math.pi * (step[:, None] * step[None, :] % LX) / LX
    cosine, sine = np.cos(theta), np.sin(theta)
    first = np.block([[cosine, sine], [-sine, cosine]])
    high, low = split_table(first)
    first = np.concatenate([high, low, high], axis=1)
    last = np.stack(
        [np.concatenate([-sine, -cosine], 1), np.concatenate([cosine, -sine], 1)],
        axis=1,
    ).reshape(2 * LX, 2 * LX) / float(LX**4)
    high, low = split_table(last)
    last = np.concatenate([high, low, high], axis=1)
    eye = np.eye(8)

    def along(table):
        cut = table.reshape(2, 16, LX)
        return np.einsum("hky,pq->hpkqy", cut, eye).reshape(256, 256)

    forth = np.concatenate([along(cosine), along(sine)], axis=1)
    back = np.concatenate([along(cosine).T, along(sine).T], axis=1)
    ends = np.zeros((128, 512), ml_dtypes.bfloat16)
    ends[:64, :192], ends[64:, :192] = first, last
    return np.concatenate(split_table(forth) + split_table(back) + (ends,), axis=0)


def cut(value):
    high = value.astype(BF16)
    low = (value - high.astype(F32)).astype(BF16)
    return high, low


def dot(left, right):
    return jnp.dot(left, right, preferred_element_type=F32)


def fine_dot(left, right_high, right_low):
    rows = left.shape[0]
    high, low = cut(left)
    both = dot(jnp.concatenate([high, low], axis=0), right_high)
    return both[:rows] + both[rows:] + dot(high, right_low)


def convolve(block, table):
    first, last = table[1024:1088, :192], table[1088:1152, :192]
    forth = table[0:256, :], table[256:512, :]
    back = table[512:768, :], table[768:1024, :]
    data = jnp.concatenate(
        [
            jnp.concatenate([block(ph, a, 0, half), block(ph, a, 1, half)], axis=0)
            for ph in range(2)
            for a in range(2)
            for half in range(2)
        ],
        axis=1,
    )
    high, low = cut(data)
    stage = dot(first, jnp.concatenate([high, high, low], axis=0))
    stage = jnp.concatenate([stage[:, 256 * i : 256 * i + 256] for i in range(4)], axis=0)
    stage = fine_dot(stage, *forth)
    prods = []
    for ph in range(2):
        parts = []
        for i in (2 * ph, 2 * ph + 1):
            re, im = stage[64 * i : 64 * i + 32], stage[64 * i + 32 : 64 * i + 64]
            parts.append((re[:, :256] + im[:, 256:], im[:, :256] - re[:, 256:]))
        (g_re, g_im), (w_re, w_im) = parts
        prods += [g_re * w_re - g_im * w_im, g_re * w_im + g_im * w_re]
    stage = fine_dot(jnp.concatenate(prods, axis=0), *back)
    wide = []
    for ph in range(2):
        re, im = stage[64 * ph : 64 * ph + 32], stage[64 * ph + 32 : 64 * ph + 64]
        wide.append(jnp.concatenate([re[:, :256] - im[:, 256:], im[:, :256] + re[:, 256:]], axis=0))
    high, low = cut(jnp.concatenate(wide, axis=1))
    return dot(last, jnp.concatenate([high, high, low], axis=0))


def kernel(
    n_ka, n_hist,
    step_hbm, g_hbm, w_hbm, gh_hbm, sh_hbm, table_hbm,
    out_ref,
    step_ref, rows_v, gh_v, sh_v, table_v,
    turned, send_rows, send_half, recv_rows, recv_half, send_sig, recv_sig, wide_sig, left_g, left_s, partial, rs_full, rs_send, rs_recv, summed,
    row_sem, table_sem, sh_sem, gh_sem, self_sem, send_sem, recv_sem,
):
    hist = lax.axis_index("hist")
    me = lax.axis_index("ka")
    slab = LX
    n_conv = slab
    convolver = me < n_conv
    barrier = pltpu.get_barrier_semaphore()

    row_copies = [
        pltpu.make_async_copy(src.at[part], rows_v.at[a, part], row_sem.at[a, part])
        for a, src in enumerate((g_hbm, w_hbm))
        for part in range(2)
    ]
    for copy in row_copies:
        copy.start()

    @pl.when(convolver)
    def _():
        def greet(i, carry):
            pl.semaphore_signal(barrier, inc=1, device_id={"ka": lax.rem(me + i, n_ka)}, device_id_type=MESH)
            return carry

        lax.fori_loop(1, n_ka, greet, 0)

    for d in range(1, n_hist):
        pl.semaphore_signal(barrier, inc=1, device_id={"hist": lax.rem(hist + d, n_hist)}, device_id_type=MESH)

    step_copy = pltpu.make_async_copy(step_hbm, step_ref, table_sem.at[0])
    table_copy = pltpu.make_async_copy(table_hbm, table_v, table_sem.at[1])
    chunks = 4
    width = 16 // chunks
    sh_copies = [
        pltpu.make_async_copy(
            sh_hbm.at[:, :, pl.ds(q * width, width)], sh_v.at[:, :, pl.ds(q * width, width)], sh_sem.at[q]
        )
        for q in range(chunks)
    ]
    gh_copies = [
        pltpu.make_async_copy(
            gh_hbm.at[:, :, pl.ds(q * width, width)], gh_v.at[:, :, pl.ds(q * width, width)], gh_sem.at[q]
        )
        for q in range(chunks)
    ]
    for copy in [step_copy] + sh_copies + [table_copy] + gh_copies:
        copy.start()

    for a in range(2):
        for part in range(2):
            r = 2 * a + part
            row_copies[r].wait()
            for ph in range(2):
                turned[2 * r + ph] = rows_v[a, part, pl.ds(128 * ph, 128), :].T
    for r in range(4):
        for ph in range(2):
            send_rows[pl.ds(4 * ph + r, slab, stride=8), :] = turned[2 * r + ph, pl.ds(slab * hist, slab), :]

    def tile(i):
        return pl.ds(pl.multiple_of(8 * i, 8), 8)

    def send_row(to, src, dst, at, which):
        pltpu.make_async_remote_copy(
            src_ref=src.at[tile(to)], dst_ref=dst.at[tile(at)], send_sem=send_sem.at[which],
            recv_sem=recv_sem.at[which], device_id={"ka": to}, device_id_type=MESH,
        ).start()

    some_rows = recv_rows.at[pl.ds(0, 8 * (n_conv - 1))]
    some_sig = recv_sig.at[:, pl.ds(0, n_conv - 1)]

    @pl.when(convolver)
    def _():
        own = pltpu.make_async_copy(send_rows.at[tile(me)], recv_rows.at[tile(me)], self_sem.at[0])
        own.start()
        pl.semaphore_wait(barrier, n_conv - 1 + n_hist - 1)

        def go(i, carry):
            send_row(lax.rem(me + i, n_conv), send_rows, recv_rows, me, 0)
            return carry

        lax.fori_loop(1, n_conv, go, 0)
        own.wait()

    @pl.when(jnp.logical_not(convolver))
    def _():
        send_half[...] = send_rows[...].astype(BF16)
        pl.semaphore_wait(barrier, n_conv + n_hist - 1)

        def go(i, carry):
            send_row(lax.rem(me + i, n_conv), send_half, recv_half, me - n_conv, 3)
            return carry

        lax.fori_loop(0, n_conv, go, 0)

    step_copy.wait()
    lane = lax.broadcasted_iota(jnp.int32, (1, 128), 1)
    place = lane // 32
    alive = (hist * slab + lane % 32) < step_ref[0]

    def spread(left, pieces):
        for part in range(2):
            for a in range(NORB):
                row = pieces(part, a, 0)
                for b in range(1, NORB):
                    row = jnp.where(place == b, pieces(part, a, b), row)
                row = jnp.where(alive, row, 0.0)
                left[part, pl.ds(a, 16, stride=8), :] = -row if part else row
                left[1 - part, pl.ds(4 + a, 16, stride=8), :] = row

    def green_piece(part, a, b):
        block = rows_v[0, part, pl.ds((4 * a + b) * 16, 16), :]
        return pltpu.roll(block, lax.rem(32 * b + 128 - 32 * hist, 128), 1)

    def left_of(left, k):
        at = pl.ds(8 * k, 8)
        return jnp.concatenate([left[0, at, :], left[1, at, :]], axis=1).astype(BF16)

    spread(left_g, green_piece)

    s_at = lax.broadcasted_iota(jnp.int32, (slab, 128), 0) + hist * slab
    t_at = lax.broadcasted_iota(jnp.int32, (slab, 128), 1)
    lower = jnp.where(s_at >= t_at, 1.0, 0.0).astype(BF16)

    def history(ref, k):
        return jnp.concatenate(
            [
                jnp.concatenate(
                    [ref[part, 4 * b + c, k] * lower for part in range(2) for b in range(NORB)], axis=0
                )
                for c in range(NORB)
            ],
            axis=1,
        )

    for q in range(chunks):
        sh_copies[q].wait()
        for kk in range(width):
            k = q * width + kk
            partial[k] = dot(left_of(left_g, k), history(sh_v, k))

    table_copy.wait()

    @pl.when(convolver)
    def _():
        pltpu.make_async_copy(some_rows, some_rows, recv_sem.at[0]).wait()
        pltpu.make_async_copy(recv_half, recv_half, recv_sem.at[3]).wait()
        recv_rows[pl.ds(8 * n_conv, 8 * n_conv), :] = recv_half[...].astype(F32)

        def block(ph, a, part, half):
            return recv_rows[pl.ds(8 * half + 4 * ph + 2 * a + part, 32, stride=16), :]

        sigma = convolve(block, table_v).astype(BF16)
        for ph in range(2):
            for half in range(2):
                at = 128 * (2 * ph + half)
                send_sig[half, ph] = sigma[:, at : at + 128].reshape(LX, 2, 128)

        def send_sigma(i, carry):
            to = 8 * (i // 8) + lax.rem(me + i, 8)

            @pl.when(to != me)
            def _():
                pltpu.make_async_remote_copy(
                    src_ref=send_sig.at[lax.rem(to, 2), :, to // 2], dst_ref=recv_sig.at[:, me],
                    send_sem=send_sem.at[1], recv_sem=recv_sem.at[1], device_id={"ka": to}, device_id_type=MESH,
                ).start()

            return carry

        lax.fori_loop(0, n_ka, send_sigma, 0)
        own = pltpu.make_async_copy(send_sig.at[lax.rem(me, 2), :, me // 2], recv_sig.at[:, me], self_sem.at[1])
        own.start()
        own.wait()
        pltpu.make_async_copy(some_sig, some_sig, recv_sem.at[1]).wait()

    @pl.when(jnp.logical_not(convolver))
    def _():
        pltpu.make_async_copy(recv_sig, recv_sig, recv_sem.at[1]).wait()

    wide_sig[...] = recv_sig[...].reshape(2, 2 * LX, 128).astype(F32)
    stacked = jnp.concatenate(
        [wide_sig[ph, pl.ds(part, 32, stride=2), :] for part in range(2) for ph in range(2)], axis=0
    ).T

    def sigma_piece(part, a, b):
        ph = a // 2
        at = ((a % 2) * 4 + b) * 16
        shift = (32 * (b - 2 * part - ph)) % 128
        rows = stacked[at : at + 16]
        return pltpu.roll(rows, shift, 1) if shift else rows

    spread(left_s, sigma_piece)

    for q in range(chunks):
        gh_copies[q].wait()
        rows = [[] for _ in range(NORB)]
        for kk in range(width):
            k = q * width + kk
            total = partial[k] + dot(left_of(left_s, k), history(gh_v, k))
            columns = [total[:, 128 * c : 128 * c + 128] for c in range(NORB)]
            for to in range(NORB):
                row = None
                for c in range(NORB):
                    shift = (32 * (c - to)) % 128
                    moved = pltpu.roll(columns[c], shift, 1) if shift else columns[c]
                    row = moved if row is None else jnp.where(place == c, moved, row)
                rows[to].append(row)
        for to in range(NORB):
            full = jnp.concatenate(rows[to], axis=0)
            rs_full[to, q] = full
            rs_send[to, q] = full.astype(BF16)
        for d in (2, 1, 3):
            to = lax.rem(hist + d, n_hist)
            pltpu.make_async_remote_copy(
                src_ref=rs_send.at[to, q], dst_ref=rs_recv.at[n_hist - 1 - d, q],
                send_sem=send_sem.at[2], recv_sem=recv_sem.at[2], device_id={"hist": to}, device_id_type=MESH,
            ).start()

    pltpu.make_async_copy(rs_recv, rs_recv, recv_sem.at[2]).wait()
    scale = 2.0 / (n_hist * slab)
    got = [rs_recv[i].reshape(128, 128).astype(F32) for i in range(3)]
    summed[...] = ((got[0] + got[1]) + (got[2] + rs_full[hist].reshape(128, 128))) * scale
    for m in range(8):
        rows = summed[pl.ds(m, 16, stride=8), :]
        for c in range(NORB):
            moved = pltpu.roll(rows, 128 - 32 * c, 1) if c else rows
            out_ref[m // 4, (m % 4) * 4 + c] = moved[:, :slab]

    pltpu.make_async_copy(rs_recv, rs_recv, send_sem.at[2]).wait()

    @pl.when(convolver)
    def _():
        pltpu.make_async_copy(some_rows, some_rows, send_sem.at[0]).wait()
        pltpu.make_async_copy(recv_sig, recv_sig, send_sem.at[1]).wait()
        pltpu.make_async_copy(some_sig, some_sig, send_sem.at[1]).wait()

    @pl.when(jnp.logical_not(convolver))
    def _():
        pltpu.make_async_copy(recv_half, recv_half, send_sem.at[3]).wait()


def per_device(n_ka, n_hist, g_row, w_row, g_hist, s_hist, step_now):
    rows = [jnp.transpose(x, (0, 1, 3, 2)).reshape(2, PAIRS * 16, 128) for x in (g_row, w_row)]
    table = jnp.asarray(tables())
    return pl.pallas_call(
        functools.partial(kernel, n_ka, n_hist),
        out_shape=jax.ShapeDtypeStruct((2, PAIRS, 16, 32), F32),
        in_specs=[pl.BlockSpec(memory_space=pl.ANY)] * 6,
        out_specs=pl.BlockSpec(memory_space=pltpu.VMEM),
        scratch_shapes=[
            pltpu.SMEM((1,), jnp.int32),
            pltpu.VMEM((2, 2, 256, 128), F32),
            pltpu.VMEM((2, 16, 16, 32, 128), BF16),
            pltpu.VMEM((2, 16, 16, 32, 128), BF16),
            pltpu.VMEM(table.shape, BF16),
            pltpu.VMEM((8, 128, 128), F32),
            pltpu.VMEM((256, 128), F32),
            pltpu.VMEM((256, 128), BF16),
            pltpu.VMEM((512, 128), F32),
            pltpu.VMEM((256, 128), BF16),
            pltpu.VMEM((2, 2, 32, 2, 128), BF16),
            pltpu.VMEM((2, 32, 2, 128), BF16),
            pltpu.VMEM((2, 64, 128), F32),
            pltpu.VMEM((2, 128, 128), F32),
            pltpu.VMEM((2, 128, 128), F32),
            pltpu.VMEM((16, 8, 512), F32),
            pltpu.VMEM((4, 4, 32, 128), F32),
            pltpu.VMEM((4, 4, 32, 128), BF16),
            pltpu.VMEM((3, 4, 32, 128), BF16),
            pltpu.VMEM((128, 128), F32),
            pltpu.SemaphoreType.DMA((2, 2)),
            pltpu.SemaphoreType.DMA((2,)),
            pltpu.SemaphoreType.DMA((4,)),
            pltpu.SemaphoreType.DMA((4,)),
            pltpu.SemaphoreType.DMA((2,)),
            pltpu.SemaphoreType.DMA((4,)),
            pltpu.SemaphoreType.DMA((4,)),
        ],
        compiler_params=pltpu.CompilerParams(
            collective_id=0, has_side_effects=True, vmem_limit_bytes=LIMIT * 1024
        ),
    )(step_now, *rows, g_hist, s_hist, table)


def solution(mesh):
    placed = (
        P(None, None, None, "ka"),
        P(None, None, None, "ka"),
        P(None, None, "ka", "hist", None),
        P(None, None, "ka", "hist", None),
        P(),
    )
    return jax.shard_map(
        functools.partial(per_device, mesh.shape["ka"], mesh.shape["hist"]),
        mesh=mesh,
        in_specs=placed,
        out_specs=P(None, None, "ka", "hist"),
        check_vma=False,
    )
```

```python
import functools
import math

import jax
import jax.numpy as jnp
import ml_dtypes
import numpy as np
from jax import lax
from jax.experimental import pallas as pl
from jax.experimental.pallas import tpu as pltpu
from jax.sharding import PartitionSpec as P

LX = 32
NORB = 4
LIMIT = 54800
PAIRS = 16
MESH = pl.DeviceIdType.MESH
F32 = jnp.float32
BF16 = jnp.bfloat16


def split_table(table):
    high = table.astype(ml_dtypes.bfloat16)
    low = (table - high.astype(np.float64)).astype(ml_dtypes.bfloat16)
    return high, low


def tables():
    step = np.arange(LX)
    theta = 2.0 * math.pi * (step[:, None] * step[None, :] % LX) / LX
    cosine, sine = np.cos(theta), np.sin(theta)
    first = np.block([[cosine, sine], [-sine, cosine]]).reshape(2 * LX, 2, 2, LX // 2)
    firsts = []
    for half in range(2):
        high, low = split_table(first[:, :, half].reshape(2 * LX, LX))
        firsts.append(np.concatenate([high, low, high], axis=1))
    last = np.stack(
        [np.concatenate([-sine, -cosine], 1), np.concatenate([cosine, -sine], 1)],
        axis=1,
    ).reshape(2 * LX, 2 * LX) / float(LX**4)
    high, low = split_table(last)
    last = np.concatenate([high, low, high], axis=1)
    eye = np.eye(8)

    def along(table):
        cut = table.reshape(2, 16, LX)
        return np.einsum("hky,pq->hpkqy", cut, eye).reshape(256, 256)

    forth = np.concatenate([along(cosine), along(sine)], axis=1)
    back = np.concatenate([along(cosine).T, along(sine).T], axis=1)
    ends = np.zeros((128, 512), ml_dtypes.bfloat16)
    ends[:64, :96], ends[:64, 128:224], ends[64:, :192] = firsts[0], firsts[1], last
    return np.concatenate(split_table(forth) + split_table(back) + (ends,), axis=0)


def cut(value):
    high = value.astype(BF16)
    low = (value - high.astype(F32)).astype(BF16)
    return high, low


def dot(left, right):
    return jnp.dot(left, right, preferred_element_type=F32)


def fine_dot(left, right_high, right_low):
    rows = left.shape[0]
    high, low = cut(left)
    both = dot(jnp.concatenate([high, low], axis=0), right_high)
    return both[:rows] + both[rows:] + dot(high, right_low)


def along_ky(stage):
    columns = []
    for i in range(4):
        re, im = stage[32 * i : 32 * i + 16], stage[32 * i + 16 : 32 * i + 32]
        columns.append(jnp.concatenate([re[:, :256] + im[:, 256:], im[:, :256] - re[:, 256:]], axis=0))
    high, low = cut(jnp.concatenate(columns, axis=1))
    return jnp.concatenate([high, high, low], axis=0)


def gather(rows, start):
    return jnp.concatenate(
        [
            jnp.concatenate([rows[pl.ds(start + 8 * half + r, 16, stride=16), :] for half in range(2)], axis=1)
            for r in range(8)
        ],
        axis=0,
    )


def early_part(rows, table):
    stage = fine_dot(gather(rows, 0), table[0:256, :], table[256:512, :])
    return dot(table[1024:1088, 0:96], along_ky(stage))


def convolve(early, rows, table):
    late = gather(rows, 256).astype(BF16)
    stage = dot(late, table[0:256, :]) + dot(late, table[256:512, :])
    stage = early + dot(table[1024:1088, 128:224], along_ky(stage))
    back = table[512:768, :], table[768:1024, :]
    last = table[1088:1152, :192]
    prods = []
    for ph in range(2):
        g, w = stage[:, 512 * ph : 512 * ph + 256], stage[:, 512 * ph + 256 : 512 * ph + 512]
        (g_re, g_im), (w_re, w_im) = (g[:32], g[32:]), (w[:32], w[32:])
        prods += [g_re * w_re - g_im * w_im, g_re * w_im + g_im * w_re]
    stage = fine_dot(jnp.concatenate(prods, axis=0), *back)
    wide = []
    for ph in range(2):
        re, im = stage[64 * ph : 64 * ph + 32], stage[64 * ph + 32 : 64 * ph + 64]
        wide.append(jnp.concatenate([re[:, :256] - im[:, 256:], im[:, :256] + re[:, 256:]], axis=0))
    high, low = cut(jnp.concatenate(wide, axis=1))
    return dot(last, jnp.concatenate([high, high, low], axis=0))


def kernel(
    n_ka, n_hist,
    step_hbm, g_hbm, w_hbm, gh_hbm, sh_hbm, table_hbm,
    out_ref,
    step_ref, rows_v, gh_v, sh_v, table_v,
    turned, send_rows, send_half, recv_rows, recv_half, send_sig, recv_sig, wide_sig, left_g, left_s, partial, rs_full, rs_send, rs_recv, summed,
    row_sem, table_sem, sh_sem, gh_sem, self_sem, send_sem, recv_sem, plane_sem, all_sem,
):
    hist = lax.axis_index("hist")
    me = lax.axis_index("ka")
    slab = LX
    n_conv = slab
    convolver = me < n_conv
    barrier = pltpu.get_barrier_semaphore()

    row_copies = [
        pltpu.make_async_copy(src.at[part], rows_v.at[a, part], row_sem.at[a, part])
        for a, src in enumerate((g_hbm, w_hbm))
        for part in range(2)
    ]
    for copy in row_copies:
        copy.start()

    @pl.when(convolver)
    def _():
        def greet(i, carry):
            to = lax.rem(me + i, n_ka)
            pl.semaphore_signal(barrier, inc=1, device_id={"ka": to}, device_id_type=MESH)
            return carry

        lax.fori_loop(1, n_ka, greet, 0)

        for d in range(1, n_hist):
            pl.semaphore_signal(barrier, inc=1, device_id={"hist": lax.rem(hist + d, n_hist)}, device_id_type=MESH)

    step_copy = pltpu.make_async_copy(step_hbm, step_ref, table_sem.at[0])
    table_copy = pltpu.make_async_copy(table_hbm, table_v, table_sem.at[1])
    chunks = 4
    width = 16 // chunks
    sh_copies = [
        pltpu.make_async_copy(
            sh_hbm.at[:, :, pl.ds(q * width, width)], sh_v.at[:, :, pl.ds(q * width, width)], sh_sem.at[q]
        )
        for q in range(chunks)
    ]
    gh_copies = [
        pltpu.make_async_copy(
            gh_hbm.at[:, :, pl.ds(q * width, width)], gh_v.at[:, :, pl.ds(q * width, width)], gh_sem.at[q]
        )
        for q in range(chunks)
    ]
    for copy in [step_copy] + sh_copies + [table_copy] + gh_copies:
        copy.start()

    for a in range(2):
        for part in range(2):
            r = 2 * a + part
            row_copies[r].wait()
            for ph in range(2):
                turned[2 * r + ph] = rows_v[a, part, pl.ds(128 * ph, 128), :].T
    for r in range(4):
        for ph in range(2):
            send_rows[pl.ds(4 * ph + r, slab, stride=8), :] = turned[2 * r + ph, pl.ds(slab * hist, slab), :]

    def tile(i):
        return pl.ds(pl.multiple_of(8 * i, 8), 8)

    def send_row(to, src, dst, at, which):
        pltpu.make_async_remote_copy(
            src_ref=src.at[tile(to)], dst_ref=dst.at[tile(at)], send_sem=send_sem.at[which],
            recv_sem=recv_sem.at[which], device_id={"ka": to}, device_id_type=MESH,
        ).start()

    some_rows = recv_rows.at[pl.ds(0, 8 * (n_conv - 1))]
    some_sig = recv_sig.at[:, pl.ds(0, n_conv - 1)]

    @pl.when(convolver)
    def _():
        own = pltpu.make_async_copy(send_rows.at[tile(me)], recv_rows.at[tile(me)], self_sem.at[0])
        own.start()
        pl.semaphore_wait(barrier, n_conv - 1 + n_hist - 1)

        def go(i, carry):
            send_row(lax.rem(me + i, n_conv), send_rows, recv_rows, me, 0)
            return carry

        lax.fori_loop(1, n_conv, go, 0)
        own.wait()

    @pl.when(jnp.logical_not(convolver))
    def _():
        send_half[...] = send_rows[...].astype(BF16)
        pl.semaphore_wait(barrier, n_conv)

        def go(i, carry):
            send_row(lax.rem(me + n_conv - i, n_conv), send_half, recv_half, me - n_conv, 3)
            return carry

        lax.fori_loop(0, n_conv, go, 0)

    step_copy.wait()
    lane = lax.broadcasted_iota(jnp.int32, (1, 128), 1)
    place = lane // 32
    alive = (hist * slab + lane % 32) < step_ref[0]

    def spread(left, pieces):
        for part in range(2):
            for a in range(NORB):
                row = pieces(part, a, 0)
                for b in range(1, NORB):
                    row = jnp.where(place == b, pieces(part, a, b), row)
                row = jnp.where(alive, row, 0.0)
                left[part, pl.ds(a, 16, stride=8), :] = -row if part else row
                left[1 - part, pl.ds(4 + a, 16, stride=8), :] = row

    def green_piece(part, a, b):
        block = rows_v[0, part, pl.ds((4 * a + b) * 16, 16), :]
        return pltpu.roll(block, lax.rem(32 * b + 128 - 32 * hist, 128), 1)

    def left_of(left, k):
        at = pl.ds(8 * k, 8)
        return jnp.concatenate([left[0, at, :], left[1, at, :]], axis=1).astype(BF16)

    spread(left_g, green_piece)

    s_at = lax.broadcasted_iota(jnp.int32, (slab, 128), 0) + hist * slab
    t_at = lax.broadcasted_iota(jnp.int32, (slab, 128), 1)
    lower = jnp.where(s_at >= t_at, 1.0, 0.0).astype(BF16)

    def history(ref, k, factor):
        return jnp.concatenate(
            [
                jnp.concatenate(
                    [factor(ref[part, 4 * b + c, k]) for part in range(2) for b in range(NORB)], axis=0
                )
                for c in range(NORB)
            ],
            axis=1,
        )

    for q in range(chunks):
        sh_copies[q].wait()
        for kk in range(width):
            k = q * width + kk
            partial[k] = dot(left_of(left_g, k), history(sh_v, k, lambda x: x * lower))

    for q in range(chunks):
        gh_copies[q].wait()

        def mask(i, carry):
            part, p = i // PAIRS, lax.rem(i, PAIRS)
            for kk in range(width):
                k = q * width + kk
                gh_v[part, p, k] = gh_v[part, p, k] * lower
            return carry

        lax.fori_loop(0, 2 * PAIRS, mask, 0)

    table_copy.wait()

    @pl.when(convolver)
    def _():
        pltpu.make_async_copy(some_rows, some_rows, recv_sem.at[0]).wait()
        early = early_part(recv_rows, table_v)
        pltpu.make_async_copy(recv_half, recv_half, recv_sem.at[3]).wait()
        for d in range(1, n_hist):
            pl.semaphore_signal(plane_sem, inc=1, device_id={"hist": lax.rem(hist + d, n_hist)}, device_id_type=MESH)
        recv_rows[pl.ds(8 * n_conv, 8 * n_conv), :] = recv_half[...].astype(F32)
        sigma = convolve(early, recv_rows, table_v).astype(BF16)
        for ph in range(2):
            for half in range(2):
                at = 128 * (2 * ph + half)
                send_sig[half, ph] = sigma[:, at : at + 128].reshape(LX, 2, 128)

        def send_sigma(i, carry):
            to = 8 * (i // 8) + lax.rem(me + i, 8)

            @pl.when(to != me)
            def _():
                pltpu.make_async_remote_copy(
                    src_ref=send_sig.at[lax.rem(to, 2), :, to // 2], dst_ref=recv_sig.at[:, me],
                    send_sem=send_sem.at[1], recv_sem=recv_sem.at[1], device_id={"ka": to}, device_id_type=MESH,
                ).start()

            return carry

        lax.fori_loop(0, n_ka, send_sigma, 0)
        own = pltpu.make_async_copy(send_sig.at[lax.rem(me, 2), :, me // 2], recv_sig.at[:, me], self_sem.at[1])
        own.start()
        pl.semaphore_wait(plane_sem, n_hist - 1)
        pl.semaphore_signal(all_sem, inc=1, device_id={"ka": me + n_conv}, device_id_type=MESH)
        own.wait()
        pltpu.make_async_copy(some_sig, some_sig, recv_sem.at[1]).wait()

    @pl.when(jnp.logical_not(convolver))
    def _():
        pltpu.make_async_copy(recv_sig, recv_sig, recv_sem.at[1]).wait()
        pl.semaphore_wait(all_sem, 1)

    wide_sig[...] = recv_sig[...].reshape(2, 2 * LX, 128).astype(F32)
    stacked = jnp.concatenate(
        [wide_sig[ph, pl.ds(part, 32, stride=2), :] for part in range(2) for ph in range(2)], axis=0
    ).T

    def sigma_piece(part, a, b):
        ph = a // 2
        at = ((a % 2) * 4 + b) * 16
        shift = (32 * (b - 2 * part - ph)) % 128
        rows = stacked[at : at + 16]
        return pltpu.roll(rows, shift, 1) if shift else rows

    spread(left_s, sigma_piece)

    for q in range(chunks):
        rows = [[] for _ in range(NORB)]
        for kk in range(width):
            k = q * width + kk
            total = partial[k] + dot(left_of(left_s, k), history(gh_v, k, lambda x: x))
            columns = [total[:, 128 * c : 128 * c + 128] for c in range(NORB)]
            for to in range(NORB):
                row = None
                for c in range(NORB):
                    shift = (32 * (c - to)) % 128
                    moved = pltpu.roll(columns[c], shift, 1) if shift else columns[c]
                    row = moved if row is None else jnp.where(place == c, moved, row)
                rows[to].append(row)
        for to in range(NORB):
            full = jnp.concatenate(rows[to], axis=0)
            rs_full[to, q] = full
            rs_send[to, q] = full.astype(BF16)
        for d in (2, 1, 3):
            to = lax.rem(hist + d, n_hist)
            pltpu.make_async_remote_copy(
                src_ref=rs_send.at[to, q], dst_ref=rs_recv.at[n_hist - 1 - d, q],
                send_sem=send_sem.at[2], recv_sem=recv_sem.at[2], device_id={"hist": to}, device_id_type=MESH,
            ).start()

    pltpu.make_async_copy(rs_recv, rs_recv, recv_sem.at[2]).wait()
    scale = 2.0 / (n_hist * slab)
    got = [rs_recv[i].reshape(128, 128).astype(F32) for i in range(3)]
    summed[...] = ((got[0] + got[1]) + (got[2] + rs_full[hist].reshape(128, 128))) * scale
    for m in range(8):
        rows = summed[pl.ds(m, 16, stride=8), :]
        for c in range(NORB):
            moved = pltpu.roll(rows, 128 - 32 * c, 1) if c else rows
            out_ref[m // 4, (m % 4) * 4 + c] = moved[:, :slab]

    pltpu.make_async_copy(rs_recv, rs_recv, send_sem.at[2]).wait()

    @pl.when(convolver)
    def _():
        pltpu.make_async_copy(some_rows, some_rows, send_sem.at[0]).wait()
        pltpu.make_async_copy(recv_sig, recv_sig, send_sem.at[1]).wait()
        pltpu.make_async_copy(some_sig, some_sig, send_sem.at[1]).wait()

    @pl.when(jnp.logical_not(convolver))
    def _():
        pltpu.make_async_copy(recv_half, recv_half, send_sem.at[3]).wait()


def per_device(n_ka, n_hist, g_row, w_row, g_hist, s_hist, step_now):
    rows = [jnp.transpose(x, (0, 1, 3, 2)).reshape(2, PAIRS * 16, 128) for x in (g_row, w_row)]
    table = jnp.asarray(tables())
    return pl.pallas_call(
        functools.partial(kernel, n_ka, n_hist),
        out_shape=jax.ShapeDtypeStruct((2, PAIRS, 16, 32), F32),
        in_specs=[pl.BlockSpec(memory_space=pl.ANY)] * 6,
        out_specs=pl.BlockSpec(memory_space=pltpu.VMEM),
        scratch_shapes=[
            pltpu.SMEM((1,), jnp.int32),
            pltpu.VMEM((2, 2, 256, 128), F32),
            pltpu.VMEM((2, 16, 16, 32, 128), BF16),
            pltpu.VMEM((2, 16, 16, 32, 128), BF16),
            pltpu.VMEM(table.shape, BF16),
            pltpu.VMEM((8, 128, 128), F32),
            pltpu.VMEM((256, 128), F32),
            pltpu.VMEM((256, 128), BF16),
            pltpu.VMEM((512, 128), F32),
            pltpu.VMEM((256, 128), BF16),
            pltpu.VMEM((2, 2, 32, 2, 128), BF16),
            pltpu.VMEM((2, 32, 2, 128), BF16),
            pltpu.VMEM((2, 64, 128), F32),
            pltpu.VMEM((2, 128, 128), F32),
            pltpu.VMEM((2, 128, 128), F32),
            pltpu.VMEM((16, 8, 512), F32),
            pltpu.VMEM((4, 4, 32, 128), F32),
            pltpu.VMEM((4, 4, 32, 128), BF16),
            pltpu.VMEM((3, 4, 32, 128), BF16),
            pltpu.VMEM((128, 128), F32),
            pltpu.SemaphoreType.DMA((2, 2)),
            pltpu.SemaphoreType.DMA((2,)),
            pltpu.SemaphoreType.DMA((4,)),
            pltpu.SemaphoreType.DMA((4,)),
            pltpu.SemaphoreType.DMA((2,)),
            pltpu.SemaphoreType.DMA((4,)),
            pltpu.SemaphoreType.DMA((4,)),
            pltpu.SemaphoreType.REGULAR,
            pltpu.SemaphoreType.REGULAR,
        ],
        compiler_params=pltpu.CompilerParams(
            collective_id=0, has_side_effects=True, vmem_limit_bytes=LIMIT * 1024
        ),
    )(step_now, *rows, g_hist, s_hist, table)


def solution(mesh):
    placed = (
        P(None, None, None, "ka"),
        P(None, None, None, "ka"),
        P(None, None, "ka", "hist", None),
        P(None, None, "ka", "hist", None),
        P(),
    )
    return jax.shard_map(
        functools.partial(per_device, mesh.shape["ka"], mesh.shape["hist"]),
        mesh=mesh,
        in_specs=placed,
        out_specs=P(None, None, "ka", "hist"),
        check_vma=False,
    )
```

```python
import functools
import math

import jax
import jax.numpy as jnp
import ml_dtypes
import numpy as np
from jax import lax
from jax.experimental import pallas as pl
from jax.experimental.pallas import tpu as pltpu
from jax.sharding import PartitionSpec as P

LX = 32
NORB = 4
LIMIT = 54800
PAIRS = 16
MESH = pl.DeviceIdType.MESH
F32 = jnp.float32
BF16 = jnp.bfloat16


def split_table(table):
    high = table.astype(ml_dtypes.bfloat16)
    low = (table - high.astype(np.float64)).astype(ml_dtypes.bfloat16)
    return high, low


def tables():
    step = np.arange(LX)
    theta = 2.0 * math.pi * (step[:, None] * step[None, :] % LX) / LX
    cosine, sine = np.cos(theta), np.sin(theta)
    first = np.block([[cosine, sine], [-sine, cosine]]).reshape(2 * LX, 2, 2, LX // 2)
    firsts = []
    for half in range(2):
        high, low = split_table(first[:, :, half].reshape(2 * LX, LX))
        firsts.append(np.concatenate([high, low, high], axis=1))
    last = np.stack(
        [np.concatenate([-sine, -cosine], 1), np.concatenate([cosine, -sine], 1)],
        axis=1,
    ).reshape(2 * LX, 2 * LX) / float(LX**4)
    high, low = split_table(last)
    last = np.concatenate([high, low, high], axis=1)
    eye = np.eye(8)

    def along(table):
        cut = table.reshape(2, 16, LX)
        return np.einsum("hky,pq->hpkqy", cut, eye).reshape(256, 256)

    forth = np.concatenate([along(cosine), along(sine)], axis=1)
    back = np.concatenate([along(cosine).T, along(sine).T], axis=1)
    ends = np.zeros((128, 512), ml_dtypes.bfloat16)
    ends[:64, :96], ends[:64, 128:224], ends[64:, :192] = firsts[0], firsts[1], last
    return np.concatenate(split_table(forth) + split_table(back) + (ends,), axis=0)


def cut(value):
    high = value.astype(BF16)
    low = (value - high.astype(F32)).astype(BF16)
    return high, low


def dot(left, right):
    return jnp.dot(left, right, preferred_element_type=F32)


def fine_dot(left, right_high, right_low):
    rows = left.shape[0]
    high, low = cut(left)
    both = dot(jnp.concatenate([high, low], axis=0), right_high)
    return both[:rows] + both[rows:] + dot(high, right_low)


def along_ky(stage):
    columns = []
    for i in range(4):
        re, im = stage[32 * i : 32 * i + 16], stage[32 * i + 16 : 32 * i + 32]
        columns.append(jnp.concatenate([re[:, :256] + im[:, 256:], im[:, :256] - re[:, 256:]], axis=0))
    high, low = cut(jnp.concatenate(columns, axis=1))
    return jnp.concatenate([high, high, low], axis=0)


def gather(rows, start):
    return jnp.concatenate(
        [
            jnp.concatenate([rows[pl.ds(start + 8 * half + r, 16, stride=16), :] for half in range(2)], axis=1)
            for r in range(8)
        ],
        axis=0,
    )


def early_part(rows, table):
    stage = fine_dot(gather(rows, 0), table[0:256, :], table[256:512, :])
    return dot(table[1024:1088, 0:96], along_ky(stage))


def convolve(early, rows, table):
    late = gather(rows, 256).astype(BF16)
    stage = dot(late, table[0:256, :]) + dot(late, table[256:512, :])
    stage = early + dot(table[1024:1088, 128:224], along_ky(stage))
    back = table[512:768, :], table[768:1024, :]
    last = table[1088:1152, :192]
    prods = []
    for ph in range(2):
        g, w = stage[:, 512 * ph : 512 * ph + 256], stage[:, 512 * ph + 256 : 512 * ph + 512]
        (g_re, g_im), (w_re, w_im) = (g[:32], g[32:]), (w[:32], w[32:])
        prods += [g_re * w_re - g_im * w_im, g_re * w_im + g_im * w_re]
    stage = fine_dot(jnp.concatenate(prods, axis=0), *back)
    wide = []
    for ph in range(2):
        re, im = stage[64 * ph : 64 * ph + 32], stage[64 * ph + 32 : 64 * ph + 64]
        wide.append(jnp.concatenate([re[:, :256] - im[:, 256:], im[:, :256] + re[:, 256:]], axis=0))
    high, low = cut(jnp.concatenate(wide, axis=1))
    return dot(last, jnp.concatenate([high, high, low], axis=0))


def kernel(
    n_ka, n_hist,
    step_hbm, g_hbm, w_hbm, gh_hbm, sh_hbm, table_hbm,
    out_ref,
    step_ref, rows_v, gh_v, sh_v, table_v,
    turned, send_rows, send_half, recv_rows, recv_half, send_sig, recv_sig, wide_sig, left_g, left_s, partial, rs_full, rs_send, rs_recv, summed,
    row_sem, table_sem, sh_sem, gh_sem, self_sem, send_sem, recv_sem, plane_sem, all_sem,
):
    hist = lax.axis_index("hist")
    me = lax.axis_index("ka")
    slab = LX
    n_conv = slab
    convolver = me < n_conv
    barrier = pltpu.get_barrier_semaphore()

    row_copies = [
        pltpu.make_async_copy(src.at[part], rows_v.at[a, part], row_sem.at[a, part])
        for a, src in enumerate((g_hbm, w_hbm))
        for part in range(2)
    ]
    for copy in row_copies:
        copy.start()

    @pl.when(convolver)
    def _():
        def greet(i, carry):
            to = lax.rem(me + i, n_ka)
            pl.semaphore_signal(barrier, inc=1, device_id={"ka": to}, device_id_type=MESH)
            return carry

        lax.fori_loop(1, n_ka, greet, 0)

        for d in range(1, n_hist):
            pl.semaphore_signal(barrier, inc=1, device_id={"hist": lax.rem(hist + d, n_hist)}, device_id_type=MESH)

    step_copy = pltpu.make_async_copy(step_hbm, step_ref, table_sem.at[0])
    table_copy = pltpu.make_async_copy(table_hbm, table_v, table_sem.at[1])
    chunks = 1
    width = 16 // chunks
    sh_copies = [
        pltpu.make_async_copy(
            sh_hbm.at[:, :, pl.ds(q * width, width)], sh_v.at[:, :, pl.ds(q * width, width)], sh_sem.at[q]
        )
        for q in range(chunks)
    ]
    gh_copies = [
        pltpu.make_async_copy(
            gh_hbm.at[:, :, pl.ds(q * width, width)], gh_v.at[:, :, pl.ds(q * width, width)], gh_sem.at[q]
        )
        for q in range(chunks)
    ]
    for copy in [step_copy] + sh_copies + [table_copy] + gh_copies:
        copy.start()

    for a in range(2):
        for part in range(2):
            r = 2 * a + part
            row_copies[r].wait()
            for ph in range(2):
                turned[2 * r + ph] = rows_v[a, part, pl.ds(128 * ph, 128), :].T
    for r in range(4):
        for ph in range(2):
            send_rows[pl.ds(4 * ph + r, slab, stride=8), :] = turned[2 * r + ph, pl.ds(slab * hist, slab), :]

    def tile(i):
        return pl.ds(pl.multiple_of(8 * i, 8), 8)

    def send_row(to, src, dst, at, which):
        pltpu.make_async_remote_copy(
            src_ref=src.at[tile(to)], dst_ref=dst.at[tile(at)], send_sem=send_sem.at[which],
            recv_sem=recv_sem.at[which], device_id={"ka": to}, device_id_type=MESH,
        ).start()

    some_rows = recv_rows.at[pl.ds(0, 8 * (n_conv - 1))]
    some_sig = recv_sig.at[:, pl.ds(0, n_conv - 1)]

    @pl.when(convolver)
    def _():
        own = pltpu.make_async_copy(send_rows.at[tile(me)], recv_rows.at[tile(me)], self_sem.at[0])
        own.start()
        pl.semaphore_wait(barrier, n_conv - 1 + n_hist - 1)

        def go(i, carry):
            send_row(lax.rem(me + i, n_conv), send_rows, recv_rows, me, 0)
            return carry

        lax.fori_loop(1, n_conv, go, 0)
        own.wait()

    @pl.when(jnp.logical_not(convolver))
    def _():
        send_half[...] = send_rows[...].astype(BF16)
        pl.semaphore_wait(barrier, n_conv)

        def go(i, carry):
            send_row(lax.rem(me + n_conv - i, n_conv), send_half, recv_half, me - n_conv, 3)
            return carry

        lax.fori_loop(0, n_conv, go, 0)

    step_copy.wait()
    lane = lax.broadcasted_iota(jnp.int32, (1, 128), 1)
    place = lane // 32
    alive = (hist * slab + lane % 32) < step_ref[0]

    def spread(left, pieces):
        for part in range(2):
            for a in range(NORB):
                row = pieces(part, a, 0)
                for b in range(1, NORB):
                    row = jnp.where(place == b, pieces(part, a, b), row)
                row = jnp.where(alive, row, 0.0)
                left[part, pl.ds(a, 16, stride=8), :] = -row if part else row
                left[1 - part, pl.ds(4 + a, 16, stride=8), :] = row

    def green_piece(part, a, b):
        block = rows_v[0, part, pl.ds((4 * a + b) * 16, 16), :]
        return pltpu.roll(block, lax.rem(32 * b + 128 - 32 * hist, 128), 1)

    def left_of(left, k):
        at = pl.ds(8 * k, 8)
        return jnp.concatenate([left[0, at, :], left[1, at, :]], axis=1).astype(BF16)

    spread(left_g, green_piece)

    s_at = lax.broadcasted_iota(jnp.int32, (slab, 128), 0) + hist * slab
    t_at = lax.broadcasted_iota(jnp.int32, (slab, 128), 1)
    lower = jnp.where(s_at >= t_at, 1.0, 0.0).astype(BF16)

    def history(ref, k, factor):
        return jnp.concatenate(
            [
                jnp.concatenate(
                    [factor(ref[part, 4 * b + c, k]) for part in range(2) for b in range(NORB)], axis=0
                )
                for c in range(NORB)
            ],
            axis=1,
        )

    for q in range(chunks):
        sh_copies[q].wait()
        for kk in range(width):
            k = q * width + kk
            partial[k] = dot(left_of(left_g, k), history(sh_v, k, lambda x: x * lower))

    for q in range(chunks):
        gh_copies[q].wait()

        def mask(i, carry):
            part, p = i // PAIRS, lax.rem(i, PAIRS)
            for kk in range(width):
                k = q * width + kk
                gh_v[part, p, k] = gh_v[part, p, k] * lower
            return carry

        lax.fori_loop(0, 2 * PAIRS, mask, 0)

    table_copy.wait()

    @pl.when(convolver)
    def _():
        pltpu.make_async_copy(some_rows, some_rows, recv_sem.at[0]).wait()
        early = early_part(recv_rows, table_v)
        pltpu.make_async_copy(recv_half, recv_half, recv_sem.at[3]).wait()
        for d in range(1, n_hist):
            pl.semaphore_signal(plane_sem, inc=1, device_id={"hist": lax.rem(hist + d, n_hist)}, device_id_type=MESH)
        recv_rows[pl.ds(8 * n_conv, 8 * n_conv), :] = recv_half[...].astype(F32)
        sigma = convolve(early, recv_rows, table_v).astype(BF16)
        for ph in range(2):
            for half in range(2):
                at = 128 * (2 * ph + half)
                send_sig[half, ph] = sigma[:, at : at + 128].reshape(LX, 2, 128)

        def send_sigma(i, carry):
            to = 8 * (i // 8) + lax.rem(me + i, 8)

            @pl.when(to != me)
            def _():
                pltpu.make_async_remote_copy(
                    src_ref=send_sig.at[lax.rem(to, 2), :, to // 2], dst_ref=recv_sig.at[:, me],
                    send_sem=send_sem.at[1], recv_sem=recv_sem.at[1], device_id={"ka": to}, device_id_type=MESH,
                ).start()

            return carry

        lax.fori_loop(0, n_ka, send_sigma, 0)
        own = pltpu.make_async_copy(send_sig.at[lax.rem(me, 2), :, me // 2], recv_sig.at[:, me], self_sem.at[1])
        own.start()
        pl.semaphore_wait(plane_sem, n_hist - 1)
        pl.semaphore_signal(all_sem, inc=1, device_id={"ka": me + n_conv}, device_id_type=MESH)
        own.wait()
        pltpu.make_async_copy(some_sig, some_sig, recv_sem.at[1]).wait()

    @pl.when(jnp.logical_not(convolver))
    def _():
        pltpu.make_async_copy(recv_sig, recv_sig, recv_sem.at[1]).wait()
        pl.semaphore_wait(all_sem, 1)

    wide_sig[...] = recv_sig[...].reshape(2, 2 * LX, 128).astype(F32)
    stacked = jnp.concatenate(
        [wide_sig[ph, pl.ds(part, 32, stride=2), :] for part in range(2) for ph in range(2)], axis=0
    ).T

    def sigma_piece(part, a, b):
        ph = a // 2
        at = ((a % 2) * 4 + b) * 16
        shift = (32 * (b - 2 * part - ph)) % 128
        rows = stacked[at : at + 16]
        return pltpu.roll(rows, shift, 1) if shift else rows

    spread(left_s, sigma_piece)

    for q in range(chunks):
        rows = [[] for _ in range(NORB)]
        for kk in range(width):
            k = q * width + kk
            total = partial[k] + dot(left_of(left_s, k), history(gh_v, k, lambda x: x))
            columns = [total[:, 128 * c : 128 * c + 128] for c in range(NORB)]
            for to in range(NORB):
                row = None
                for c in range(NORB):
                    shift = (32 * (c - to)) % 128
                    moved = pltpu.roll(columns[c], shift, 1) if shift else columns[c]
                    row = moved if row is None else jnp.where(place == c, moved, row)
                rows[to].append(row)
        for to in range(NORB):
            full = jnp.concatenate(rows[to], axis=0)
            rs_full[to, q] = full
            rs_send[to, q] = full.astype(BF16)
        for d in (2, 1, 3):
            to = lax.rem(hist + d, n_hist)
            pltpu.make_async_remote_copy(
                src_ref=rs_send.at[to, q], dst_ref=rs_recv.at[n_hist - 1 - d, q],
                send_sem=send_sem.at[2], recv_sem=recv_sem.at[2], device_id={"hist": to}, device_id_type=MESH,
            ).start()

    pltpu.make_async_copy(rs_recv, rs_recv, recv_sem.at[2]).wait()
    scale = 2.0 / (n_hist * slab)
    got = [rs_recv[i].reshape(128, 128).astype(F32) for i in range(3)]
    summed[...] = ((got[0] + got[1]) + (got[2] + rs_full[hist].reshape(128, 128))) * scale
    for m in range(8):
        rows = summed[pl.ds(m, 16, stride=8), :]
        for c in range(NORB):
            moved = pltpu.roll(rows, 128 - 32 * c, 1) if c else rows
            out_ref[m // 4, (m % 4) * 4 + c] = moved[:, :slab]

    pltpu.make_async_copy(rs_recv, rs_recv, send_sem.at[2]).wait()

    @pl.when(convolver)
    def _():
        pltpu.make_async_copy(some_rows, some_rows, send_sem.at[0]).wait()
        pltpu.make_async_copy(recv_sig, recv_sig, send_sem.at[1]).wait()
        pltpu.make_async_copy(some_sig, some_sig, send_sem.at[1]).wait()

    @pl.when(jnp.logical_not(convolver))
    def _():
        pltpu.make_async_copy(recv_half, recv_half, send_sem.at[3]).wait()


def per_device(n_ka, n_hist, g_row, w_row, g_hist, s_hist, step_now):
    rows = [jnp.transpose(x, (0, 1, 3, 2)).reshape(2, PAIRS * 16, 128) for x in (g_row, w_row)]
    table = jnp.asarray(tables())
    return pl.pallas_call(
        functools.partial(kernel, n_ka, n_hist),
        out_shape=jax.ShapeDtypeStruct((2, PAIRS, 16, 32), F32),
        in_specs=[pl.BlockSpec(memory_space=pl.ANY)] * 6,
        out_specs=pl.BlockSpec(memory_space=pltpu.VMEM),
        scratch_shapes=[
            pltpu.SMEM((1,), jnp.int32),
            pltpu.VMEM((2, 2, 256, 128), F32),
            pltpu.VMEM((2, 16, 16, 32, 128), BF16),
            pltpu.VMEM((2, 16, 16, 32, 128), BF16),
            pltpu.VMEM(table.shape, BF16),
            pltpu.VMEM((8, 128, 128), F32),
            pltpu.VMEM((256, 128), F32),
            pltpu.VMEM((256, 128), BF16),
            pltpu.VMEM((512, 128), F32),
            pltpu.VMEM((256, 128), BF16),
            pltpu.VMEM((2, 2, 32, 2, 128), BF16),
            pltpu.VMEM((2, 32, 2, 128), BF16),
            pltpu.VMEM((2, 64, 128), F32),
            pltpu.VMEM((2, 128, 128), F32),
            pltpu.VMEM((2, 128, 128), F32),
            pltpu.VMEM((16, 8, 512), F32),
            pltpu.VMEM((4, 1, 128, 128), F32),
            pltpu.VMEM((4, 1, 128, 128), BF16),
            pltpu.VMEM((3, 1, 128, 128), BF16),
            pltpu.VMEM((128, 128), F32),
            pltpu.SemaphoreType.DMA((2, 2)),
            pltpu.SemaphoreType.DMA((2,)),
            pltpu.SemaphoreType.DMA((1,)),
            pltpu.SemaphoreType.DMA((1,)),
            pltpu.SemaphoreType.DMA((2,)),
            pltpu.SemaphoreType.DMA((4,)),
            pltpu.SemaphoreType.DMA((4,)),
            pltpu.SemaphoreType.REGULAR,
            pltpu.SemaphoreType.REGULAR,
        ],
        compiler_params=pltpu.CompilerParams(
            collective_id=0, has_side_effects=True, vmem_limit_bytes=LIMIT * 1024
        ),
    )(step_now, *rows, g_hist, s_hist, table)


def solution(mesh):
    placed = (
        P(None, None, None, "ka"),
        P(None, None, None, "ka"),
        P(None, None, "ka", "hist", None),
        P(None, None, "ka", "hist", None),
        P(),
    )
    return jax.shard_map(
        functools.partial(per_device, mesh.shape["ka"], mesh.shape["hist"]),
        mesh=mesh,
        in_specs=placed,
        out_specs=P(None, None, "ka", "hist"),
        check_vma=False,
    )
```

```python
import functools
import math

import jax
import jax.numpy as jnp
import ml_dtypes
import numpy as np
from jax import lax
from jax.experimental import pallas as pl
from jax.experimental.pallas import tpu as pltpu
from jax.sharding import PartitionSpec as P

LX = 32
NORB = 4
LIMIT = 54800
PAIRS = 16
MESH = pl.DeviceIdType.MESH
F32 = jnp.float32
BF16 = jnp.bfloat16


def split_table(table):
    high = table.astype(ml_dtypes.bfloat16)
    low = (table - high.astype(np.float64)).astype(ml_dtypes.bfloat16)
    return high, low


def tables():
    step = np.arange(LX)
    theta = 2.0 * math.pi * (step[:, None] * step[None, :] % LX) / LX
    cosine, sine = np.cos(theta), np.sin(theta)
    first = np.block([[cosine, sine], [-sine, cosine]]).reshape(2 * LX, 2, 2, LX // 2)
    firsts = []
    for half in range(2):
        high, low = split_table(first[:, :, half].reshape(2 * LX, LX))
        firsts.append(np.concatenate([high, low, high], axis=1))
    last = np.stack(
        [np.concatenate([-sine, -cosine], 1), np.concatenate([cosine, -sine], 1)],
        axis=1,
    ).reshape(2 * LX, 2 * LX) / float(LX**4)
    high, low = split_table(last)
    last = np.concatenate([high, low, high], axis=1)
    eye = np.eye(8)

    def along(table):
        cut = table.reshape(2, 16, LX)
        return np.einsum("hky,pq->hpkqy", cut, eye).reshape(256, 256)

    forth = np.concatenate([along(cosine), along(sine)], axis=1)
    back = np.concatenate([along(cosine).T, along(sine).T], axis=1)
    ends = np.zeros((128, 512), ml_dtypes.bfloat16)
    ends[:64, :96], ends[:64, 128:224], ends[64:, :192] = firsts[0], firsts[1], last
    return np.concatenate(split_table(forth) + split_table(back) + (ends,), axis=0)


def cut(value):
    high = value.astype(BF16)
    low = (value - high.astype(F32)).astype(BF16)
    return high, low


def dot(left, right):
    return jnp.dot(left, right, preferred_element_type=F32)


def fine_dot(left, right_high, right_low):
    rows = left.shape[0]
    high, low = cut(left)
    both = dot(jnp.concatenate([high, low], axis=0), right_high)
    return both[:rows] + both[rows:] + dot(high, right_low)


def along_ky(stage):
    columns = []
    for i in range(4):
        re, im = stage[32 * i : 32 * i + 16], stage[32 * i + 16 : 32 * i + 32]
        columns.append(jnp.concatenate([re[:, :256] + im[:, 256:], im[:, :256] - re[:, 256:]], axis=0))
    high, low = cut(jnp.concatenate(columns, axis=1))
    return jnp.concatenate([high, high, low], axis=0)


def gather(rows, start):
    return jnp.concatenate(
        [
            jnp.concatenate([rows[pl.ds(start + 8 * half + r, 16, stride=16), :] for half in range(2)], axis=1)
            for r in range(8)
        ],
        axis=0,
    )


def early_part(rows, table):
    stage = fine_dot(gather(rows, 0), table[0:256, :], table[256:512, :])
    return dot(table[1024:1088, 0:96], along_ky(stage))


def convolve(early, rows, table):
    late = gather(rows, 256).astype(BF16)
    stage = dot(late, table[0:256, :]) + dot(late, table[256:512, :])
    stage = early + dot(table[1024:1088, 128:224], along_ky(stage))
    back = table[512:768, :], table[768:1024, :]
    last = table[1088:1152, :192]
    prods = []
    for ph in range(2):
        g, w = stage[:, 512 * ph : 512 * ph + 256], stage[:, 512 * ph + 256 : 512 * ph + 512]
        (g_re, g_im), (w_re, w_im) = (g[:32], g[32:]), (w[:32], w[32:])
        prods += [g_re * w_re - g_im * w_im, g_re * w_im + g_im * w_re]
    stage = fine_dot(jnp.concatenate(prods, axis=0), *back)
    wide = []
    for ph in range(2):
        re, im = stage[64 * ph : 64 * ph + 32], stage[64 * ph + 32 : 64 * ph + 64]
        wide.append(jnp.concatenate([re[:, :256] - im[:, 256:], im[:, :256] + re[:, 256:]], axis=0))
    high, low = cut(jnp.concatenate(wide, axis=1))
    return dot(last, jnp.concatenate([high, high, low], axis=0))


def kernel(
    n_ka, n_hist,
    step_hbm, g_hbm, w_hbm, gh_hbm, sh_hbm, table_hbm,
    out_ref,
    step_ref, rows_v, gh_v, sh_v, table_v,
    turned, send_rows, send_half, recv_rows, recv_half, send_sig, recv_sig, wide_sig, left_g, left_s, partial, rs_full, rs_send, rs_recv, summed,
    row_sem, table_sem, sh_sem, gh_sem, self_sem, send_sem, recv_sem, plane_sem, all_sem,
):
    hist = lax.axis_index("hist")
    me = lax.axis_index("ka")
    slab = LX
    n_conv = slab
    convolver = me < n_conv
    barrier = pltpu.get_barrier_semaphore()

    row_copies = [
        pltpu.make_async_copy(src.at[part], rows_v.at[a, part], row_sem.at[a, part])
        for a, src in enumerate((g_hbm, w_hbm))
        for part in range(2)
    ]
    for copy in row_copies:
        copy.start()

    @pl.when(convolver)
    def _():
        def greet(i, carry):
            to = lax.rem(me + i, n_ka)
            pl.semaphore_signal(barrier, inc=1, device_id={"ka": to}, device_id_type=MESH)
            return carry

        lax.fori_loop(1, n_ka, greet, 0)

        for d in range(1, n_hist):
            pl.semaphore_signal(barrier, inc=1, device_id={"hist": lax.rem(hist + d, n_hist)}, device_id_type=MESH)

    step_copy = pltpu.make_async_copy(step_hbm, step_ref, table_sem.at[0])
    table_copy = pltpu.make_async_copy(table_hbm, table_v, table_sem.at[1])
    chunks = 1
    width = 16 // chunks
    sh_copies = [
        pltpu.make_async_copy(
            sh_hbm.at[:, :, pl.ds(q * width, width)], sh_v.at[:, :, pl.ds(q * width, width)], sh_sem.at[q]
        )
        for q in range(chunks)
    ]
    gh_copies = [
        pltpu.make_async_copy(
            gh_hbm.at[:, :, pl.ds(q * width, width)], gh_v.at[:, :, pl.ds(q * width, width)], gh_sem.at[q]
        )
        for q in range(chunks)
    ]
    for copy in [step_copy] + sh_copies + [table_copy] + gh_copies:
        copy.start()

    for a in range(2):
        for part in range(2):
            r = 2 * a + part
            row_copies[r].wait()
            for ph in range(2):
                turned[2 * r + ph] = rows_v[a, part, pl.ds(128 * ph, 128), :].T
    for r in range(4):
        for ph in range(2):
            send_rows[pl.ds(4 * ph + r, slab, stride=8), :] = turned[2 * r + ph, pl.ds(slab * hist, slab), :]

    def tile(i):
        return pl.ds(pl.multiple_of(8 * i, 8), 8)

    def send_row(to, src, dst, at, which):
        pltpu.make_async_remote_copy(
            src_ref=src.at[tile(to)], dst_ref=dst.at[tile(at)], send_sem=send_sem.at[which],
            recv_sem=recv_sem.at[which], device_id={"ka": to}, device_id_type=MESH,
        ).start()

    some_rows = recv_rows.at[pl.ds(0, 8 * (n_conv - 1))]
    some_sig = recv_sig.at[:, pl.ds(0, n_conv - 1)]

    @pl.when(convolver)
    def _():
        own = pltpu.make_async_copy(send_rows.at[tile(me)], recv_rows.at[tile(me)], self_sem.at[0])
        own.start()
        pl.semaphore_wait(barrier, n_conv - 1 + n_hist - 1)

        def go(i, carry):
            send_row(lax.rem(me + i, n_conv), send_rows, recv_rows, me, 0)
            return carry

        lax.fori_loop(1, n_conv, go, 0)
        own.wait()

    @pl.when(jnp.logical_not(convolver))
    def _():
        send_half[...] = send_rows[...].astype(BF16)
        pl.semaphore_wait(barrier, n_conv)

        def go(i, carry):
            send_row(8 * lax.rem(me // 8 + 8 - i // 8, 4) + lax.rem(me + i, 8), send_half, recv_half, me - n_conv, 3)
            return carry

        lax.fori_loop(0, n_conv, go, 0)

    step_copy.wait()
    lane = lax.broadcasted_iota(jnp.int32, (1, 128), 1)
    place = lane // 32
    alive = (hist * slab + lane % 32) < step_ref[0]

    def spread(left, pieces):
        for part in range(2):
            for a in range(NORB):
                row = pieces(part, a, 0)
                for b in range(1, NORB):
                    row = jnp.where(place == b, pieces(part, a, b), row)
                row = jnp.where(alive, row, 0.0)
                left[part, pl.ds(a, 16, stride=8), :] = -row if part else row
                left[1 - part, pl.ds(4 + a, 16, stride=8), :] = row

    def green_piece(part, a, b):
        block = rows_v[0, part, pl.ds((4 * a + b) * 16, 16), :]
        return pltpu.roll(block, lax.rem(32 * b + 128 - 32 * hist, 128), 1)

    def left_of(left, k):
        at = pl.ds(8 * k, 8)
        return jnp.concatenate([left[0, at, :], left[1, at, :]], axis=1).astype(BF16)

    spread(left_g, green_piece)

    s_at = lax.broadcasted_iota(jnp.int32, (slab, 128), 0) + hist * slab
    t_at = lax.broadcasted_iota(jnp.int32, (slab, 128), 1)
    lower = jnp.where(s_at >= t_at, 1.0, 0.0).astype(BF16)

    def history(ref, k, factor):
        return jnp.concatenate(
            [
                jnp.concatenate(
                    [factor(ref[part, 4 * b + c, k]) for part in range(2) for b in range(NORB)], axis=0
                )
                for c in range(NORB)
            ],
            axis=1,
        )

    for q in range(chunks):
        sh_copies[q].wait()
        for kk in range(width):
            k = q * width + kk
            partial[k] = dot(left_of(left_g, k), history(sh_v, k, lambda x: x * lower))

    for q in range(chunks):
        gh_copies[q].wait()

        def mask(i, carry):
            part, p = i // PAIRS, lax.rem(i, PAIRS)
            for kk in range(width):
                k = q * width + kk
                gh_v[part, p, k] = gh_v[part, p, k] * lower
            return carry

        lax.fori_loop(0, 2 * PAIRS, mask, 0)

    table_copy.wait()

    @pl.when(convolver)
    def _():
        pltpu.make_async_copy(some_rows, some_rows, recv_sem.at[0]).wait()
        early = early_part(recv_rows, table_v)
        pltpu.make_async_copy(recv_half, recv_half, recv_sem.at[3]).wait()
        for d in range(1, n_hist):
            pl.semaphore_signal(plane_sem, inc=1, device_id={"hist": lax.rem(hist + d, n_hist)}, device_id_type=MESH)
        recv_rows[pl.ds(8 * n_conv, 8 * n_conv), :] = recv_half[...].astype(F32)
        sigma = convolve(early, recv_rows, table_v).astype(BF16)
        for ph in range(2):
            for half in range(2):
                at = 128 * (2 * ph + half)
                send_sig[half, ph] = sigma[:, at : at + 128].reshape(LX, 2, 128)

        def send_sigma(i, carry):
            to = 8 * (i // 8) + lax.rem(me + i, 8)

            @pl.when(to != me)
            def _():
                pltpu.make_async_remote_copy(
                    src_ref=send_sig.at[lax.rem(to, 2), :, to // 2], dst_ref=recv_sig.at[:, me],
                    send_sem=send_sem.at[1], recv_sem=recv_sem.at[1], device_id={"ka": to}, device_id_type=MESH,
                ).start()

            return carry

        lax.fori_loop(0, n_ka, send_sigma, 0)
        own = pltpu.make_async_copy(send_sig.at[lax.rem(me, 2), :, me // 2], recv_sig.at[:, me], self_sem.at[1])
        own.start()
        pl.semaphore_wait(plane_sem, n_hist - 1)
        pl.semaphore_signal(all_sem, inc=1, device_id={"ka": me + n_conv}, device_id_type=MESH)
        own.wait()
        pltpu.make_async_copy(some_sig, some_sig, recv_sem.at[1]).wait()

    @pl.when(jnp.logical_not(convolver))
    def _():
        pltpu.make_async_copy(recv_sig, recv_sig, recv_sem.at[1]).wait()
        pl.semaphore_wait(all_sem, 1)

    wide_sig[...] = recv_sig[...].reshape(2, 2 * LX, 128).astype(F32)
    stacked = jnp.concatenate(
        [wide_sig[ph, pl.ds(part, 32, stride=2), :] for part in range(2) for ph in range(2)], axis=0
    ).T

    def sigma_piece(part, a, b):
        ph = a // 2
        at = ((a % 2) * 4 + b) * 16
        shift = (32 * (b - 2 * part - ph)) % 128
        rows = stacked[at : at + 16]
        return pltpu.roll(rows, shift, 1) if shift else rows

    spread(left_s, sigma_piece)

    for q in range(chunks):
        rows = [[] for _ in range(NORB)]
        for kk in range(width):
            k = q * width + kk
            total = partial[k] + dot(left_of(left_s, k), history(gh_v, k, lambda x: x))
            columns = [total[:, 128 * c : 128 * c + 128] for c in range(NORB)]
            for to in range(NORB):
                row = None
                for c in range(NORB):
                    shift = (32 * (c - to)) % 128
                    moved = pltpu.roll(columns[c], shift, 1) if shift else columns[c]
                    row = moved if row is None else jnp.where(place == c, moved, row)
                rows[to].append(row)
        for to in range(NORB):
            full = jnp.concatenate(rows[to], axis=0)
            rs_full[to, q] = full
            rs_send[to, q] = full.astype(BF16)
        for d in (2, 1, 3):
            to = lax.rem(hist + d, n_hist)
            pltpu.make_async_remote_copy(
                src_ref=rs_send.at[to, q], dst_ref=rs_recv.at[n_hist - 1 - d, q],
                send_sem=send_sem.at[2], recv_sem=recv_sem.at[2], device_id={"hist": to}, device_id_type=MESH,
            ).start()

    pltpu.make_async_copy(rs_recv, rs_recv, recv_sem.at[2]).wait()
    scale = 2.0 / (n_hist * slab)
    got = [rs_recv[i].reshape(128, 128).astype(F32) for i in range(3)]
    summed[...] = ((got[0] + got[1]) + (got[2] + rs_full[hist].reshape(128, 128))) * scale
    for m in range(8):
        rows = summed[pl.ds(m, 16, stride=8), :]
        for c in range(NORB):
            moved = pltpu.roll(rows, 128 - 32 * c, 1) if c else rows
            out_ref[m // 4, (m % 4) * 4 + c] = moved[:, :slab]

    pltpu.make_async_copy(rs_recv, rs_recv, send_sem.at[2]).wait()

    @pl.when(convolver)
    def _():
        pltpu.make_async_copy(some_rows, some_rows, send_sem.at[0]).wait()
        pltpu.make_async_copy(recv_sig, recv_sig, send_sem.at[1]).wait()
        pltpu.make_async_copy(some_sig, some_sig, send_sem.at[1]).wait()

    @pl.when(jnp.logical_not(convolver))
    def _():
        pltpu.make_async_copy(recv_half, recv_half, send_sem.at[3]).wait()


def per_device(n_ka, n_hist, g_row, w_row, g_hist, s_hist, step_now):
    rows = [jnp.transpose(x, (0, 1, 3, 2)).reshape(2, PAIRS * 16, 128) for x in (g_row, w_row)]
    table = jnp.asarray(tables())
    return pl.pallas_call(
        functools.partial(kernel, n_ka, n_hist),
        out_shape=jax.ShapeDtypeStruct((2, PAIRS, 16, 32), F32),
        in_specs=[pl.BlockSpec(memory_space=pl.ANY)] * 6,
        out_specs=pl.BlockSpec(memory_space=pltpu.VMEM),
        scratch_shapes=[
            pltpu.SMEM((1,), jnp.int32),
            pltpu.VMEM((2, 2, 256, 128), F32),
            pltpu.VMEM((2, 16, 16, 32, 128), BF16),
            pltpu.VMEM((2, 16, 16, 32, 128), BF16),
            pltpu.VMEM(table.shape, BF16),
            pltpu.VMEM((8, 128, 128), F32),
            pltpu.VMEM((256, 128), F32),
            pltpu.VMEM((256, 128), BF16),
            pltpu.VMEM((512, 128), F32),
            pltpu.VMEM((256, 128), BF16),
            pltpu.VMEM((2, 2, 32, 2, 128), BF16),
            pltpu.VMEM((2, 32, 2, 128), BF16),
            pltpu.VMEM((2, 64, 128), F32),
            pltpu.VMEM((2, 128, 128), F32),
            pltpu.VMEM((2, 128, 128), F32),
            pltpu.VMEM((16, 8, 512), F32),
            pltpu.VMEM((4, 1, 128, 128), F32),
            pltpu.VMEM((4, 1, 128, 128), BF16),
            pltpu.VMEM((3, 1, 128, 128), BF16),
            pltpu.VMEM((128, 128), F32),
            pltpu.SemaphoreType.DMA((2, 2)),
            pltpu.SemaphoreType.DMA((2,)),
            pltpu.SemaphoreType.DMA((1,)),
            pltpu.SemaphoreType.DMA((1,)),
            pltpu.SemaphoreType.DMA((2,)),
            pltpu.SemaphoreType.DMA((4,)),
            pltpu.SemaphoreType.DMA((4,)),
            pltpu.SemaphoreType.REGULAR,
            pltpu.SemaphoreType.REGULAR,
        ],
        compiler_params=pltpu.CompilerParams(
            collective_id=0, has_side_effects=True, vmem_limit_bytes=LIMIT * 1024
        ),
    )(step_now, *rows, g_hist, s_hist, table)


def solution(mesh):
    placed = (
        P(None, None, None, "ka"),
        P(None, None, None, "ka"),
        P(None, None, "ka", "hist", None),
        P(None, None, "ka", "hist", None),
        P(),
    )
    return jax.shard_map(
        functools.partial(per_device, mesh.shape["ka"], mesh.shape["hist"]),
        mesh=mesh,
        in_specs=placed,
        out_specs=P(None, None, "ka", "hist"),
        check_vma=False,
    )
```
